1024 devices in a mesh: tm: 128 (over z, x_lo, core), op: 8 (over x_hi, y).
Axes of the slice: x: 4 (x_hi: 2, x_lo: 2; x = x_hi * 2 + x_lo), y: 4, z: 32, core: 2. Of those that a mesh axis runs over, the one named last changes fastest.
Arguments:
- sink_fields: bfloat16 [128, 2, 2, 512, 512], P('tm', None, None, 'op'), may hold values from -0.1875 to 0.1875
- source_fields: bfloat16 [128, 2, 2, 512, 512], P('tm', None, None, 'op'), may hold values from -0.1875 to 0.1875
- source_live: int32 [128], P('tm'), may hold values 0 or 1
- chain_factors: int32 [128, 4], replicated, may hold values from 0 to 1
- chain_target: int32 [128], replicated, may hold values from 0 to 15
Outputs:
- correlators: float32 [2, 16, 2], replicated
The draws below stay inside these ranges and needn't reach their ends.
All inputs are finite; a program needn't handle non-finite values. No bound on the sum of `source_live` on one device may be relied on, other than what follows from the above.
Results may differ from the reference program's by a relative error of at most 0.0039.
Values may be sent and summed in bfloat16 or wider, within the bound.
A program may use at most 32 MiB of HBM per device.

```python
import math
import jax
import jax.numpy as jnp
from jax import lax

E = 512
NF = 2
WIN = 2
NCH = 128
NCORR = 16
NT = 128


def place_ends(array, stream_key, smallest, largest):
    place = [jax.random.randint(jax.random.fold_in(stream_key, axis), (), 0, length) for axis, length in enumerate(array.shape)]
    longest = array.shape.index(max(array.shape))
    neighbour = place[:longest] + [(place[longest] + 1) % array.shape[longest]] + place[longest + 1:]
    return array.at[tuple(place)].set(smallest).at[tuple(neighbour)].set(largest)


def block_scale(rng, shape, shards, smallest, largest):
    loudness = 1.0
    for axis_at, parts in shards:
        steps = jax.random.uniform(jax.random.fold_in(jax.random.fold_in(rng, 6), axis_at), (parts,), jnp.float32, smallest / len(shards), largest / len(shards))
        loudness = loudness * jnp.repeat(jnp.exp(steps), shape[axis_at] // parts).reshape((-1,) + (1,) * (len(shape) - 1 - axis_at))
    return loudness


def noise(key, shape, scale, reach, pieces=(), kind=jnp.bfloat16):
    factor_of = block_scale(key, shape, pieces, -0.22, 0.18) if pieces else 1.0
    array = jax.random.normal(key, shape, jnp.float32) * scale * factor_of
    return jnp.minimum(jnp.maximum(array, -reach), reach).astype(kind)


def setup_inputs(seed: int = 0) -> dict:
    keys = jax.random.split(jax.random.key(seed), 6)
    sink_fields = noise(keys[0], (NT, NF, 2, E, E), (2 * E) ** -0.5, 0.1875, ((0, 128), (3, 8)))
    source_fields = noise(keys[1], (NT, NF, 2, E, E), (2 * E) ** -0.5, 0.1875, ((0, 128), (3, 8)))
    source_live = place_ends((jax.random.randint(keys[2], (NT,), 0, 4) < 3).astype(jnp.int32), jax.random.fold_in(keys[2], 1), 0, 1)
    chain_factors = place_ends(jax.random.randint(keys[3], (NCH, 4), 0, NF), jax.random.fold_in(keys[3], 1), 0, NF - 1).astype(jnp.int32)
    chain_target = place_ends(jax.random.randint(keys[4], (NCH,), 0, NCORR), jax.random.fold_in(keys[4], 1), 0, NCORR - 1).astype(jnp.int32)
    return dict(sink_fields=sink_fields, source_fields=source_fields, source_live=source_live, chain_factors=chain_factors, chain_target=chain_target)


def stacked_block(planes):
    real_part = planes[..., 0, :, :]
    imag_part = planes[..., 1, :, :]
    upper_half = jnp.concatenate([real_part, imag_part], -1)
    lower_half = jnp.concatenate([-imag_part, real_part], -1)
    return jnp.concatenate([upper_half, lower_half], -2)

def reference(sink_fields, source_fields, source_live, chain_factors, chain_target):
    pair_count = NF * NF
    chain_codes = (chain_factors[:, 0] * NF + chain_factors[:, 1]) * pair_count + chain_factors[:, 2] * NF + chain_factors[:, 3]
    chain_onehot = (chain_codes[:, None] == jnp.arange(pair_count * pair_count, dtype=jnp.int32)[None, :]).astype(jnp.float32)
    target_onehot = (chain_target[:, None] == jnp.arange(NCORR, dtype=jnp.int32)[None, :]).astype(jnp.float32)
    selector = jnp.dot(target_onehot.T, chain_onehot, precision=lax.Precision.HIGHEST)
    results = []
    for separation in range(1, WIN + 1):

        def per_source(source_time):
            sink_time = ((source_time + separation) % NT).astype(jnp.int32)
            sink_now = lax.dynamic_index_in_dim(sink_fields, sink_time, 0, keepdims=False).astype(jnp.float32)
            source_now = lax.dynamic_index_in_dim(source_fields, source_time, 0, keepdims=False).astype(jnp.float32)
            left_stack = jnp.concatenate([sink_now[:, 0], sink_now[:, 1]], -1)
            products = jnp.einsum('aix,bxy->abiy', left_stack, stacked_block(source_now), precision=lax.Precision.HIGHEST)
            rounded = lax.optimization_barrier(products.astype(jnp.bfloat16)).astype(jnp.float32)
            flattened = rounded.reshape(pair_count, E, 2 * E)
            real_block = flattened[..., :E]
            imag_block = flattened[..., E:]
            real_trace = jnp.einsum('pij,qji->pq', real_block, real_block, precision=lax.Precision.HIGHEST) - jnp.einsum('pij,qji->pq', imag_block, imag_block, precision=lax.Precision.HIGHEST)
            imag_trace = jnp.einsum('pij,qji->pq', real_block, imag_block, precision=lax.Precision.HIGHEST) + jnp.einsum('pij,qji->pq', imag_block, real_block, precision=lax.Precision.HIGHEST)
            traces = jnp.stack([real_trace.reshape(-1), imag_trace.reshape(-1)])
            weight = lax.dynamic_index_in_dim(source_live, source_time, 0, keepdims=False).astype(jnp.float32)
            return weight * traces
        summed = lax.optimization_barrier(jnp.sum(lax.map(per_source, jnp.arange(NT, dtype=jnp.int32)), axis=0))
        results.append(jnp.dot(summed, selector.T, precision=lax.Precision.HIGHEST))
    return jnp.stack(results, -1) / math.sqrt(NT)
```

```python
import functools
import math

import jax
import jax.numpy as jnp
from jax import lax
from jax.experimental import pallas as pl
from jax.experimental.pallas import tpu as pltpu
from jax.sharding import PartitionSpec as P

WIN = 2
NF = 2
NCORR = 16
PLANE = 4
MESH = pl.DeviceIdType.MESH


def kernel(
    ntm,
    nop,
    sink_hbm,
    source_hbm,
    live_hbm,
    factors_hbm,
    target_hbm,
    out_ref,
    rfull,
    sbuf,
    prod,
    psend,
    recv,
    row,
    row_op,
    row_lo,
    row_z,
    live,
    factors,
    target,
    local_sem,
    gather_send,
    gather_recv,
    shift_send,
    shift_recv,
    block_send,
    block_recv,
    red_send,
    red_recv,
    token,
):
    nz = ntm // PLANE
    rows = source_hbm.shape[3]
    width = source_hbm.shape[4]
    tm = lax.axis_index("tm")
    op = lax.axis_index("op")
    zz = tm // PLANE
    lo = tm - zz * PLANE

    def tm_at(offset):
        return lax.rem(tm + (offset + ntm), ntm)

    def op_at(offset):
        return lax.rem(op + (offset + nop), nop)

    recv[...] = jnp.zeros_like(recv)

    barrier = pltpu.get_barrier_semaphore()
    near = [o for d in range(1, PLANE + 1) for o in (d, -d)]
    for offset in near:
        pl.semaphore_signal(barrier, inc=1, device_id=(tm_at(offset), op), device_id_type=MESH)
    for d in range(1, nop):
        pl.semaphore_signal(barrier, inc=1, device_id=(tm, op_at(d)), device_id_type=MESH)

    my_rows = pl.ds(pl.multiple_of(op * rows, rows), rows)
    local = [
        pltpu.make_async_copy(source_hbm.at[0], rfull.at[:, :, my_rows, :], local_sem.at[0]),
        pltpu.make_async_copy(live_hbm, live, local_sem.at[1]),
        pltpu.make_async_copy(factors_hbm, factors, local_sem.at[2]),
        pltpu.make_async_copy(target_hbm, target, local_sem.at[3]),
    ]
    for copy in local:
        copy.start()

    pl.semaphore_wait(barrier, len(near) + nop - 1)

    gathers = []
    for d in range(1, nop):
        gathers.append(
            pltpu.make_async_remote_copy(
                src_ref=source_hbm.at[0],
                dst_ref=rfull.at[:, :, my_rows, :],
                send_sem=gather_send.at[d],
                recv_sem=gather_recv.at[d],
                device_id=(tm, op_at(d)),
                device_id_type=MESH,
            )
        )
    shifts = []
    for w in range(WIN):
        shifts.append(
            pltpu.make_async_remote_copy(
                src_ref=sink_hbm.at[0],
                dst_ref=sbuf.at[w],
                send_sem=shift_send.at[w],
                recv_sem=shift_recv.at[w],
                device_id=(tm_at(-1 - w), op),
                device_id_type=MESH,
            )
        )
    for copy in gathers + shifts:
        copy.start()

    known = 1
    step = 0
    while known < nz // 2:
        for way in (1, -1):
            pl.semaphore_signal(
                token.at[step],
                inc=1,
                device_id=(tm_at(way * PLANE * known), op),
                device_id_type=MESH,
            )
        pl.semaphore_wait(token.at[step], 2)
        known *= 2
        step += 1

    for copy in local:
        copy.wait()

    fac = factors[...]
    codes = fac[0:1] * (2 * NF * NF) + fac[1:2] * (NF * NF) + fac[2:3] * NF + fac[3:4]
    swapped = fac[2:3] * (2 * NF * NF) + fac[3:4] * (NF * NF) + fac[0:1] * NF + fac[1:2]
    chains = codes.shape[1]
    lane_row = lax.broadcasted_iota(jnp.int32, (128, chains), 0)
    lane_ab = lax.rem(lane_row // 8, 4)
    lane_cd = lax.rem(lane_row, 4)
    lane_code = lane_ab * 4 + lane_cd
    hits = (codes == lane_code).astype(jnp.float32) + (swapped == lane_code).astype(jnp.float32)
    target_hits = (
        target[...] == lax.broadcasted_iota(jnp.int32, (NCORR, chains), 0)
    ).astype(jnp.float32)
    selector = lax.dot_general(
        target_hits.astype(jnp.bfloat16),
        hits.astype(jnp.bfloat16),
        (((1,), (1,)), ((), ())),
        preferred_element_type=jnp.float32,
    )
    weight = live[0].astype(jnp.float32)

    for copy in gathers + shifts:
        copy.wait()

    lhs_real = sbuf[:, :, 0].reshape(WIN * NF * rows, width)
    lhs_imag = sbuf[:, :, 1].reshape(WIN * NF * rows, width)
    half = min(256, width)
    for n in range(width // half):
        cols = slice(n * half, (n + 1) * half)
        for b in range(NF):
            right_real = rfull[b, 0, :, cols]
            right_imag = rfull[b, 1, :, cols]

            def mul(x, y):
                return jnp.dot(x, y, preferred_element_type=jnp.float32)

            real = mul(lhs_real, right_real) - mul(lhs_imag, right_imag)
            imag = mul(lhs_real, right_imag) + mul(lhs_imag, right_real)
            prod[:, 0, :, b, :, cols] = real.astype(jnp.bfloat16).reshape(WIN, NF, rows, half)
            prod[:, 1, :, b, :, cols] = imag.astype(jnp.bfloat16).reshape(WIN, NF, rows, half)

    left = lax.broadcasted_iota(jnp.int32, (rows, 128), 1) < rows
    for w in range(WIN):
        for part in range(2):
            for a in range(NF):
                for tile in range(width // 128):
                    lanes = slice(tile * 128, (tile + 1) * 128)
                    first = prod[w, part, a, 0, :, lanes].astype(jnp.float32)
                    second = prod[w, part, a, 1, :, lanes].astype(jnp.float32)
                    even = jnp.where(left, first, pltpu.roll(second, rows, 1))
                    odd = jnp.where(left, pltpu.roll(first, rows, 1), second)
                    psend[2 * tile, w, a * 2 + part] = even.astype(jnp.bfloat16)
                    psend[2 * tile + 1, w, a * 2 + part] = odd.astype(jnp.bfloat16)

    blocks = []
    for d in range(1, nop // 2):
        dest = op_at(-d)
        blocks.append(
            pltpu.make_async_remote_copy(
                src_ref=psend.at[dest],
                dst_ref=recv.at[:, :, my_rows, :],
                send_sem=block_send.at[d],
                recv_sem=block_recv.at[d],
                device_id=(tm, dest),
                device_id_type=MESH,
            )
        )
    facing = op_at(nop // 2)
    facing_win = facing // (nop // 2)
    blocks.append(
        pltpu.make_async_remote_copy(
            src_ref=psend.at[facing, facing_win],
            dst_ref=recv.at[facing_win, :, my_rows, :],
            send_sem=block_send.at[nop // 2],
            recv_sem=block_recv.at[nop // 2],
            device_id=(tm, facing),
            device_id_type=MESH,
        )
    )
    for copy in blocks:
        copy.start()
    recv[:, :, my_rows, :] = psend[op] * jnp.bfloat16(0.5)
    for copy in blocks:
        copy.wait()

    total = jnp.zeros((8, 128), jnp.float32)
    place_row = lax.broadcasted_iota(jnp.int32, (8, 128), 0)
    place_lane = lax.broadcasted_iota(jnp.int32, (8, 128), 1)
    diagonal = lax.broadcasted_iota(jnp.int32, (rows, 256), 0) == lax.rem(
        lax.broadcasted_iota(jnp.int32, (rows, 256), 1), rows
    )
    for w in range(WIN):
        own = prod[w].reshape(2 * NF * NF * rows, width)
        for c in range(NF):
            right = jnp.concatenate([recv[w, 2 * c], recv[w, 2 * c + 1]], axis=-1)
            square = jnp.dot(own, right, preferred_element_type=jnp.float32)
            kept = jnp.where(diagonal, square.reshape(2 * NF * NF, rows, 256), 0.0).sum(axis=1)
            with_real = kept[:, :128]
            with_imag = kept[:, 128:]
            real = with_real[:4] - with_imag[4:]
            imag = with_imag[:4] + with_real[4:]
            both = jnp.concatenate([real, imag], axis=0)
            for d in range(NF):
                inside = (place_lane >= d * 64) & (place_lane < (d + 1) * 64)
                value = jnp.where(inside, both, 0.0).sum(axis=1, keepdims=True)
                slot = place_lane == place_row * 8 + (w * 4 + c * 2 + d)
                total = total + jnp.where(slot, value, 0.0)
    row[...] = total.sum(axis=0, keepdims=True) * weight

    def exchange(buffer, me, peers, sem):
        buffer[me] = row[...]
        copies = []
        for peer, device in peers:
            copies.append(
                pltpu.make_async_remote_copy(
                    src_ref=row,
                    dst_ref=buffer.at[me],
                    send_sem=red_send.at[sem],
                    recv_sem=red_recv.at[sem],
                    device_id=device,
                    device_id_type=MESH,
                )
            )
        for copy in copies:
            copy.start()
        many = buffer.at[pl.ds(0, len(peers))]
        pltpu.make_async_copy(many, many, red_recv.at[sem]).wait()
        pltpu.make_async_copy(many, many, red_send.at[sem]).wait()
        row[...] = buffer[...].sum(axis=0)

    exchange(row_op, op, [(d, (tm, op_at(d))) for d in range(1, nop)], 0)
    exchange(
        row_lo,
        lo,
        [(d, (zz * PLANE + lax.rem(lo + d, PLANE), op)) for d in range(1, PLANE)],
        1,
    )
    exchange(row_z, zz, [(d, (tm_at(d * PLANE), op)) for d in range(1, nz)], 2)

    spread = row[...] * selector * (1.0 / math.sqrt(ntm))
    lane = lax.broadcasted_iota(jnp.int32, (NCORR, 128), 1)
    for part in range(2):
        for w in range(WIN):
            mine = (lane // 32 == part) & (lax.rem(lane // 4, 2) == w)
            out_ref[part, :, w : w + 1] = jnp.where(mine, spread, 0.0).sum(axis=1, keepdims=True)


def per_device(ntm, nop, sink, source, live, factors, target):
    rows, width = sink.shape[3], sink.shape[4]
    chains = target.shape[0]
    any_space = pl.BlockSpec(memory_space=pl.ANY)
    dma = pltpu.SemaphoreType.DMA
    return pl.pallas_call(
        functools.partial(kernel, ntm, nop),
        out_shape=jax.ShapeDtypeStruct((2, NCORR, WIN), jnp.float32),
        in_specs=[any_space] * 5,
        out_specs=pl.BlockSpec(memory_space=pltpu.VMEM),
        scratch_shapes=[
            pltpu.VMEM((NF, 2, width, width), jnp.bfloat16),
            pltpu.VMEM((WIN, NF, 2, rows, width), jnp.bfloat16),
            pltpu.VMEM((WIN, 2, NF, NF, rows, width), jnp.bfloat16),
            pltpu.VMEM((nop, WIN, 2 * NF, rows, 128), jnp.bfloat16),
            pltpu.VMEM((WIN, 2 * NF, width, 128), jnp.bfloat16),
            pltpu.VMEM((1, 128), jnp.float32),
            pltpu.VMEM((nop, 1, 128), jnp.float32),
            pltpu.VMEM((PLANE, 1, 128), jnp.float32),
            pltpu.VMEM((ntm // PLANE, 1, 128), jnp.float32),
            pltpu.SMEM((1,), jnp.int32),
            pltpu.VMEM((4, chains), jnp.int32),
            pltpu.VMEM((1, chains), jnp.int32),
            dma((4,)),
            dma((nop,)),
            dma((nop,)),
            dma((WIN,)),
            dma((WIN,)),
            dma((nop,)),
            dma((nop,)),
            dma((3,)),
            dma((3,)),
            pltpu.SemaphoreType.REGULAR((8,)),
        ],
        compiler_params=pltpu.CompilerParams(
            collective_id=0, has_side_effects=True, vmem_limit_bytes=48 << 20
        ),
        name="correlate",
    )(sink, source, live, factors.T, target.reshape(1, chains))


def solution(mesh):
    ntm, nop = mesh.shape["tm"], mesh.shape["op"]
    return jax.shard_map(
        functools.partial(per_device, ntm, nop),
        mesh=mesh,
        in_specs=(
            P("tm", None, None, "op", None),
            P("tm", None, None, "op", None),
            P("tm"),
            P(),
            P(),
        ),
        out_specs=P(),
        check_vma=False,
    )
```

```python
import functools
import math

import jax
import jax.numpy as jnp
from jax import lax
from jax.experimental import pallas as pl
from jax.experimental.pallas import tpu as pltpu
from jax.sharding import PartitionSpec as P

WIN = 2
NF = 2
NCORR = 16
NX = 4
MESH = pl.DeviceIdType.MESH


def kernel(
    ntm,
    nop,
    sink_hbm,
    source_hbm,
    live_hbm,
    factors_hbm,
    target_hbm,
    out_ref,
    rfull,
    sbuf,
    prod,
    recv,
    row_plane,
    row_z,
    plane,
    line,
    live,
    factors,
    target,
    local_sem,
    source_send,
    source_recv,
    sink_send,
    sink_recv,
    ring_send,
    ring_recv,
    pair_send,
    pair_recv,
    block_send,
    block_recv,
    red_send,
    red_recv,
    token,
):
    nz, ny = ntm // NX, nop // 2
    rows = source_hbm.shape[3]
    tm, op = lax.axis_index("tm"), lax.axis_index("op")
    z, hi = tm // NX, op // ny
    lo, core = lax.rem(tm // 2, 2), lax.rem(tm, 2)
    x, y = hi * 2 + lo, lax.rem(op, ny)
    here = lo * 2 + core

    def at(base, offset, count):
        return lax.rem(base + (offset % count), count)

    def device(z_at, x_at, core_at, y_at):
        return (z_at * NX + lax.rem(x_at, 2) * 2 + core_at, x_at // 2 * ny + y_at)

    def send(src, dst, send_sem, recv_sem, where):
        return pltpu.make_async_remote_copy(
            src_ref=src,
            dst_ref=dst,
            send_sem=send_sem,
            recv_sem=recv_sem,
            device_id=where,
            device_id_type=MESH,
        )

    def arrived(ref, sem):
        pltpu.make_async_copy(ref, ref, sem).wait()

    recv[2] = jnp.zeros(recv.shape[1:], recv.dtype)

    barrier = pltpu.get_barrier_semaphore()
    greeted = 0
    spot = x * 2 + core
    for dz in (0, 1, -1):
        for k in range(1 if dz == 0 else 0, 2 * NX):
            other = at(spot, k, 2 * NX)
            where = device(at(z, dz, nz), other // 2, lax.rem(other, 2), y)
            pl.semaphore_signal(barrier, inc=1, device_id=where, device_id_type=MESH)
            greeted += 1
    for dy in range(1, ny):
        for k in range(2):
            where = device(z, x, at(core, k, 2), at(y, dy, ny))
            pl.semaphore_signal(barrier, inc=1, device_id=where, device_id_type=MESH)
            greeted += 1

    local = [
        pltpu.make_async_copy(live_hbm, live, local_sem.at[0]),
        pltpu.make_async_copy(factors_hbm, factors, local_sem.at[1]),
        pltpu.make_async_copy(target_hbm, target, local_sem.at[2]),
    ]
    for copy in local:
        copy.start()

    pl.semaphore_wait(barrier, greeted)

    def rows_of(index):
        return pl.ds(pl.multiple_of(index * rows, rows), rows)

    outgoing = []

    def launch(src, dst, send_sem, recv_sem, where, mine):
        copy = send(src, dst, send_sem, recv_sem, where)

        @pl.when(mine)
        def _():
            pltpu.make_async_copy(src, dst, recv_sem).start()

        @pl.when(jnp.logical_not(mine))
        def _():
            copy.start()

        outgoing.append((copy, mine))

    for b in range(NF):
        launch(
            source_hbm.at[0, b],
            rfull.at[b, :, rows_of(op), :],
            source_send.at[b],
            source_recv.at[hi],
            device(z, here, b, y),
            (here == x) & (core == b),
        )
    for w in range(WIN):
        back = here - (w + 1)
        wrap = (back < 0).astype(jnp.int32)
        column = back + wrap * NX
        launch(
            sink_hbm.at[0],
            sbuf.at[:, :, rows_of(hi), :],
            sink_send.at[w],
            sink_recv.at[hi],
            device(lax.rem(z + nz - wrap, nz), column, w, y),
            (wrap == 0) & (column == x) & (core == w),
        )

    ring = []
    pairs = []
    left_y, right_y, far_y = at(y, -1, ny), at(y, 1, ny), at(y, 2, ny)

    def chunk(field, half, y_at):
        return rfull.at[field, :, rows_of(half * ny + y_at), :]

    def pass_on(half, y_at, way):
        ref = chunk(core, half, y_at)
        copy = send(
            ref,
            ref,
            ring_send.at[len(ring)],
            ring_recv.at[half * ny + y_at],
            device(z, x, core, at(y, way, ny)),
        )
        copy.start()
        ring.append(copy)

    def share(half, y_at):
        ref = chunk(core, half, y_at)
        index = half * ny + y_at
        copy = send(
            ref,
            ref,
            pair_send.at[index],
            pair_recv.at[index],
            device(z, x, 1 - core, y),
        )
        copy.start()
        pairs.append(copy)

    tokens = []
    known = 1
    while known < nz // 2:
        tokens.append(known)
        known *= 2

    def token_send(step):
        if step < len(tokens):
            for way in (1, -1):
                where = device(at(z, way * tokens[step], nz), x, core, y)
                pl.semaphore_signal(token.at[step], inc=1, device_id=where, device_id_type=MESH)

    def token_wait(step):
        if step < len(tokens):
            pl.semaphore_wait(token.at[step], 2)

    token_send(0)
    first, second = hi, 1 - hi
    arrived(chunk(core, first, y), source_recv.at[first])
    pass_on(first, y, 1)
    pass_on(first, y, -1)
    share(first, y)
    arrived(chunk(core, second, y), source_recv.at[second])
    pass_on(second, y, -1)
    pass_on(second, y, 1)
    share(second, y)
    token_wait(0)
    token_send(1)

    def from_ring(half, y_at, way):
        arrived(chunk(core, half, y_at), ring_recv.at[half * ny + y_at])
        if way:
            pass_on(half, y_at, way)
        share(half, y_at)

    from_ring(first, left_y, 1)
    from_ring(first, right_y, 0)
    from_ring(second, right_y, -1)
    from_ring(second, left_y, 0)
    token_wait(1)
    token_send(2)

    for copy in local:
        copy.wait()
    fac = factors[...]
    codes = fac[1:2] * 8 + fac[0:1] * 4 + fac[3:4] * 2 + fac[2:3]
    swapped = fac[3:4] * 8 + fac[2:3] * 4 + fac[1:2] * 2 + fac[0:1]
    chains = codes.shape[1]
    lane_row = lax.broadcasted_iota(jnp.int32, (128, chains), 0)
    lane_code = lax.rem(lane_row // 8, 4) * 4 + lax.rem(lane_row, 4)
    hits = (codes == lane_code).astype(jnp.float32) + (swapped == lane_code).astype(jnp.float32)
    target_hits = (
        target[...] == lax.broadcasted_iota(jnp.int32, (NCORR, chains), 0)
    ).astype(jnp.float32)
    selector = lax.dot_general(
        target_hits.astype(jnp.bfloat16),
        hits.astype(jnp.bfloat16),
        (((1,), (1,)), ((), ())),
        preferred_element_type=jnp.float32,
    )
    flag = live[0].astype(jnp.float32)

    from_ring(first, far_y, 0)
    from_ring(second, far_y, 0)
    for half in range(2):
        arrived(sbuf.at[:, :, rows_of(half), :], sink_recv.at[half])

    tall = 2 * rows
    lhs_real = sbuf[:, 0].reshape(NF * tall, nop * rows)
    lhs_imag = sbuf[:, 1].reshape(NF * tall, nop * rows)
    left = lax.broadcasted_iota(jnp.int32, (NF * tall, 128), 1) < 64

    def mul(a, b):
        return jnp.dot(a, b, preferred_element_type=jnp.float32)

    def multiply(b):
        for n in range(2):
            low, high = slice(n * 128, n * 128 + 128), slice(n * 128 + 256, n * 128 + 384)
            right_real = jnp.concatenate([rfull[b, 0, :, low], rfull[b, 0, :, high]], axis=-1)
            right_imag = jnp.concatenate([rfull[b, 1, :, low], rfull[b, 1, :, high]], axis=-1)
            real = mul(lhs_real, right_real) - mul(lhs_imag, right_imag)
            imag = mul(lhs_real, right_imag) + mul(lhs_imag, right_real)
            for part, value in enumerate((real, imag)):
                one, two = value[:, :128], value[:, 128:]
                even = jnp.where(left, one, pltpu.roll(two, 64, 1)).astype(jnp.bfloat16)
                odd = jnp.where(left, pltpu.roll(one, 64, 1), two).astype(jnp.bfloat16)
                prod[2 * n, b, part] = even.reshape(NF, tall, 128)
                prod[2 * n + 1, b, part] = odd.reshape(NF, tall, 128)

    step_y = 1 - 2 * core
    giver_y = lax.rem(y + step_y + ny, ny)
    taker_y = lax.rem(y - step_y + ny, ny)
    gives_far = lax.rem(y // 2 + core, 2) == 1
    blocks = []
    far_blocks = []

    def give(b, index):
        near_copy = send(
            prod.at[taker_y, b],
            recv.at[1, b],
            block_send.at[index],
            block_recv.at[index],
            device(z, x, core, taker_y),
        )
        far_copy = send(
            prod.at[far_y, b],
            recv.at[2, b],
            block_send.at[2 + index],
            block_recv.at[2 + index],
            device(z, x, core, far_y),
        )

        @pl.when(gives_far)
        def _():
            far_copy.start()

        near_copy.start()
        blocks.append(near_copy)
        far_blocks.append(far_copy)

    multiply(core)
    for half in range(2):
        for y_at in range(ny):
            arrived(chunk(1 - core, half, y_at), pair_recv.at[half * ny + y_at])
    give(core, 0)
    multiply(1 - core)
    token_wait(2)
    token_send(3)
    give(1 - core, 1)
    recv[0] = prod[y] * jnp.bfloat16(0.5)
    for copy in blocks:
        copy.wait_recv()

    @pl.when(jnp.logical_not(gives_far))
    def _():
        for copy in far_blocks:
            copy.wait_recv()

    order = [(part, b, a) for part in range(2) for b in range(NF) for a in range(NF)]
    own = jnp.concatenate(
        [
            jnp.concatenate([prod[at_y, b, part, a] for part, b, a in order], axis=0)
            for at_y in (y, giver_y, far_y)
        ],
        axis=1,
    )
    place_row = lax.broadcasted_iota(jnp.int32, (8, 128), 0)
    place_lane = lax.broadcasted_iota(jnp.int32, (8, 128), 1)
    diagonal = lax.broadcasted_iota(jnp.int32, (tall, 256), 0) == lax.rem(
        lax.broadcasted_iota(jnp.int32, (tall, 256), 1), 128
    )
    total = jnp.zeros((8, 128), jnp.float32)
    for d in range(NF):
        for c in range(NF):
            right = jnp.concatenate(
                [
                    jnp.concatenate([recv[slot, d, 0, c], recv[slot, d, 1, c]], axis=1)
                    for slot in range(3)
                ],
                axis=0,
            )
            square = mul(own, right).reshape(8, tall, 256)
            kept = jnp.where(diagonal, square, 0.0).sum(axis=1)
            with_real, with_imag = kept[:, :128], kept[:, 128:]
            real = with_real[:4] - with_imag[4:]
            imag = with_imag[:4] + with_real[4:]
            value = jnp.concatenate([real, imag], axis=0).sum(axis=1, keepdims=True)
            slot_at = place_lane == place_row * 8 + (core * 4 + d * 2 + c)
            total = total + jnp.where(slot_at, value, 0.0)
    lane = lax.broadcasted_iota(jnp.int32, (1, 128), 1)
    row_plane[...] = total.sum(axis=0, keepdims=True) + jnp.where(
        lane == 64 + here, flag * (1.0 / nop), 0.0
    )

    def exchange(buffer, me, source, peers, index):
        buffer[me] = source[...]
        for where in peers:
            send(source, buffer.at[me], red_send.at[index], red_recv.at[index], where).start()
        many = buffer.at[pl.ds(0, len(peers))]
        arrived(many, red_recv.at[index])

    def around(d, n):
        return min(d, n - d)

    spots = [(dx, dy, k) for dx in range(NX) for dy in range(ny) for k in range(2)][1:]
    spots.sort(key=lambda s: -(around(s[0], NX) + around(s[1], ny)))
    exchange(
        plane,
        x * nop + core * ny + y,
        row_plane,
        [device(z, at(x, dx, NX), at(core, k, 2), at(y, dy, ny)) for dx, dy, k in spots],
        0,
    )
    sums = [plane[j * nop : (j + 1) * nop].sum(axis=0) for j in range(NX)]
    flags = sums[0] + sums[1] + sums[2] + sums[3]
    weighted = jnp.zeros((1, 128), jnp.float32)
    for j in range(NX):
        alive = jnp.where(lane == 64 + j, flags, 0.0).sum(axis=1, keepdims=True)
        weighted = weighted + alive * sums[j]
    row_z[...] = weighted

    token_wait(3)
    hops = sorted(range(1, nz), key=lambda d: -around(d, nz))
    exchange(line, z, row_z, [device(at(z, d, nz), x, core, y) for d in hops], 1)
    everything = line[...].sum(axis=0)

    pick_row = lax.broadcasted_iota(jnp.int32, (8, 128), 0)
    pick_lane = lax.broadcasted_iota(jnp.int32, (8, 128), 1)
    picked = (pick_lane // 32 == pick_row // 2) & (
        lax.rem(pick_lane // 4, 2) == lax.rem(pick_row, 2)
    )
    spread = jnp.where(picked, everything * (1.0 / math.sqrt(ntm)), 0.0)
    result = lax.dot_general(
        spread,
        selector,
        (((1,), (1,)), ((), ())),
        precision=lax.Precision.HIGHEST,
        preferred_element_type=jnp.float32,
    )
    out_ref[...] = result[:4]

    for copy, mine in outgoing:

        @pl.when(jnp.logical_not(mine))
        def _(copy=copy):
            copy.wait_send()

    for copy in ring + pairs + blocks:
        copy.wait_send()

    @pl.when(gives_far)
    def _():
        for copy in far_blocks:
            copy.wait_send()

    arrived(plane.at[pl.ds(0, len(spots))], red_send.at[0])
    arrived(line.at[pl.ds(0, len(hops))], red_send.at[1])


def per_device(ntm, nop, sink, source, live, factors, target):
    rows, width = sink.shape[3], sink.shape[4]
    chains = target.shape[0]
    hbm = pl.BlockSpec(memory_space=pltpu.HBM)
    dma = pltpu.SemaphoreType.DMA
    out = pl.pallas_call(
        functools.partial(kernel, ntm, nop),
        out_shape=jax.ShapeDtypeStruct((2 * WIN, NCORR), jnp.float32),
        in_specs=[hbm] * 5,
        out_specs=pl.BlockSpec(memory_space=pltpu.VMEM),
        scratch_shapes=[
            pltpu.VMEM((NF, 2, width, width), jnp.bfloat16),
            pltpu.VMEM((NF, 2, 2 * rows, width), jnp.bfloat16),
            pltpu.VMEM((nop // 2, NF, 2, NF, 2 * rows, 128), jnp.bfloat16),
            pltpu.VMEM((3, NF, 2, NF, 2 * rows, 128), jnp.bfloat16),
            pltpu.VMEM((1, 128), jnp.float32),
            pltpu.VMEM((1, 128), jnp.float32),
            pltpu.VMEM((NX * nop, 1, 128), jnp.float32),
            pltpu.VMEM((ntm // NX, 1, 128), jnp.float32),
            pltpu.SMEM((1,), jnp.int32),
            pltpu.VMEM((4, chains), jnp.int32),
            pltpu.VMEM((1, chains), jnp.int32),
            dma((3,)),
            dma((NF,)),
            dma((2,)),
            dma((WIN,)),
            dma((2,)),
            dma((6,)),
            dma((nop,)),
            dma((nop,)),
            dma((nop,)),
            dma((4,)),
            dma((4,)),
            dma((2,)),
            dma((2,)),
            pltpu.SemaphoreType.REGULAR((8,)),
        ],
        compiler_params=pltpu.CompilerParams(
            collective_id=0, has_side_effects=True, vmem_limit_bytes=67043328
        ),
        name="correlate",
    )(sink, source, live, factors.T, target.reshape(1, chains))
    return jnp.moveaxis(out.reshape(2, WIN, NCORR), 1, 2)


def solution(mesh):
    ntm, nop = mesh.shape["tm"], mesh.shape["op"]
    return jax.shard_map(
        functools.partial(per_device, ntm, nop),
        mesh=mesh,
        in_specs=(
            P("tm", None, None, "op", None),
            P("tm", None, None, "op", None),
            P("tm"),
            P(),
            P(),
        ),
        out_specs=P(),
        check_vma=False,
    )
```

```python
import functools
import math

import jax
import jax.numpy as jnp
from jax import lax
from jax.experimental import pallas as pl
from jax.experimental.pallas import tpu as pltpu
from jax.sharding import PartitionSpec as P

WIN = 2
NF = 2
NCORR = 16
NX = 4
MESH = pl.DeviceIdType.MESH


def kernel(
    ntm,
    nop,
    sink_hbm,
    source_hbm,
    live,
    factors_hbm,
    target_hbm,
    out_ref,
    rfull,
    sbuf,
    prod,
    recv,
    row_plane,
    row_z,
    plane,
    line,
    factors,
    target,
    local_sem,
    source_send,
    source_recv,
    sink_send,
    sink_recv,
    ring_send,
    ring_recv,
    pair_send,
    pair_recv,
    block_send,
    block_recv,
    red_send,
    red_recv,
    token,
):
    nz, ny = ntm // NX, nop // 2
    rows = source_hbm.shape[3]
    tm, op = lax.axis_index("tm"), lax.axis_index("op")
    z, hi = tm // NX, op // ny
    lo, core = lax.rem(tm // 2, 2), lax.rem(tm, 2)
    x, y = hi * 2 + lo, lax.rem(op, ny)
    here = lo * 2 + core

    def at(base, offset, count):
        return lax.rem(base + (offset % count), count)

    def device(z_at, x_at, core_at, y_at):
        return (z_at * NX + lax.rem(x_at, 2) * 2 + core_at, x_at // 2 * ny + y_at)

    def send(src, dst, send_sem, recv_sem, where):
        return pltpu.make_async_remote_copy(
            src_ref=src,
            dst_ref=dst,
            send_sem=send_sem,
            recv_sem=recv_sem,
            device_id=where,
            device_id_type=MESH,
        )

    def arrived(ref, sem):
        pltpu.make_async_copy(ref, ref, sem).wait()

    barrier = pltpu.get_barrier_semaphore()

    def greet(where):
        pl.semaphore_signal(barrier, inc=1, device_id=where, device_id_type=MESH)

    shifts = []
    greeted = 2 * NX - 1 + 2 * (ny - 1) + 2
    for w in range(WIN):
        back = here - (w + 1)
        wrap = (back < 0).astype(jnp.int32)
        column = back + wrap * NX
        where = device(lax.rem(z + nz - wrap, nz), column, w, y)
        shifts.append((where, (wrap == 0) & (column == x) & (core == w)))
        greeted = greeted + wrap

        @pl.when(wrap == 1)
        def _(where=where):
            greet(where)

    sink_time = x + core + 1
    greeted = greeted + jnp.where(sink_time >= NX, 2, 0)

    @pl.when(sink_time >= NX)
    def _():
        for half in range(2):
            greet((at(z, 1, nz) * NX + sink_time - NX, half * ny + y))

    spot = x * 2 + core
    for k in range(1, 2 * NX):
        other = at(spot, k, 2 * NX)
        greet(device(z, other // 2, lax.rem(other, 2), y))
    for dy in range(1, ny):
        for k in range(2):
            greet(device(z, x, at(core, k, 2), at(y, dy, ny)))
    for dz in (1, -1):
        greet(device(at(z, dz, nz), x, core, y))

    local = [
        pltpu.make_async_copy(factors_hbm, factors, local_sem.at[0]),
        pltpu.make_async_copy(target_hbm, target, local_sem.at[1]),
    ]
    for copy in local:
        copy.start()

    pl.semaphore_wait(barrier, greeted)

    def rows_of(index):
        return pl.ds(pl.multiple_of(index * rows, rows), rows)

    outgoing = []

    def launch(src, dst, send_sem, recv_sem, where, mine):
        copy = send(src, dst, send_sem, recv_sem, where)

        @pl.when(mine)
        def _():
            pltpu.make_async_copy(src, dst, recv_sem).start()

        @pl.when(jnp.logical_not(mine))
        def _():
            copy.start()

        outgoing.append((copy, mine))

    for b in range(NF):
        for part in range(2):
            launch(
                source_hbm.at[0, b, part],
                rfull.at[b, part, rows_of(op), :],
                source_send.at[b * 2 + part],
                source_recv.at[b * 2 + hi],
                device(z, here, part, y),
                (here == x) & (core == part),
            )
    for w, (where, mine) in enumerate(shifts):
        launch(
            sink_hbm.at[0],
            sbuf.at[:, :, rows_of(hi), :],
            sink_send.at[w],
            sink_recv.at[hi],
            where,
            mine,
        )

    ring = []
    pairs = []
    left_y, right_y, far_y = at(y, -1, ny), at(y, 1, ny), at(y, 2, ny)

    def chunk(b, part, half, y_at):
        return rfull.at[b, part, rows_of(half * ny + y_at), :]

    def pass_on(b, half, y_at, way):
        ref = chunk(b, core, half, y_at)
        copy = send(
            ref,
            ref,
            ring_send.at[len(ring)],
            ring_recv.at[b * nop + half * ny + y_at],
            device(z, x, core, at(y, way, ny)),
        )
        copy.start()
        ring.append(copy)

    def share(b, half, y_at):
        ref = chunk(b, core, half, y_at)
        index = b * nop + half * ny + y_at
        copy = send(
            ref,
            ref,
            pair_send.at[index],
            pair_recv.at[index],
            device(z, x, 1 - core, y),
        )
        copy.start()
        pairs.append(copy)

    step_y = 1 - 2 * core
    giver_y = lax.rem(y + step_y + ny, ny)
    taker_y = lax.rem(y - step_y + ny, ny)
    gives_far = lax.rem(y // 2 + core, 2) == 1
    tokens = []
    known = 1
    while known < nz // 2:
        tokens.append(known)
        known *= 2

    def token_send(step):
        if step < len(tokens):
            for way in (1, -1):
                where = device(at(z, way * tokens[step], nz), x, core, y)
                pl.semaphore_signal(token.at[step], inc=1, device_id=where, device_id_type=MESH)

    def token_wait(step):
        if step < len(tokens):
            pl.semaphore_wait(token.at[step], 2)

    token_send(0)
    first, second = hi, 1 - hi

    def from_source(b, half, way):
        arrived(chunk(b, core, half, y), source_recv.at[b * 2 + half])
        pass_on(b, half, y, way)
        pass_on(b, half, y, -way)
        share(b, half, y)

    def from_ring(b, half, y_at, way):
        arrived(chunk(b, core, half, y_at), ring_recv.at[b * nop + half * ny + y_at])
        if way:
            pass_on(b, half, y_at, way)
        share(b, half, y_at)

    from_source(0, first, 1)
    from_source(0, second, -1)
    from_source(1, first, 1)
    from_ring(0, first, left_y, 1)
    from_ring(0, second, right_y, -1)
    from_source(1, second, -1)
    token_wait(0)
    token_send(1)
    from_ring(0, first, right_y, 0)
    from_ring(0, second, left_y, 0)
    from_ring(1, first, left_y, 1)
    from_ring(1, second, right_y, -1)

    @pl.when(gives_far)
    def _():
        recv[2] = jnp.zeros(recv.shape[1:], recv.dtype)

    for copy in local:
        copy.wait()
    fac = factors[...]
    codes = fac[1:2] * 8 + fac[0:1] * 4 + fac[3:4] * 2 + fac[2:3]
    swapped = fac[3:4] * 8 + fac[2:3] * 4 + fac[1:2] * 2 + fac[0:1]
    chains = codes.shape[1]
    lane_row = lax.broadcasted_iota(jnp.int32, (128, chains), 0)
    lane_code = lax.rem(lane_row // 8, 4) * 4 + lax.rem(lane_row, 4)
    hits = (codes == lane_code).astype(jnp.float32) + (swapped == lane_code).astype(jnp.float32)
    target_hits = (
        target[...] == lax.broadcasted_iota(jnp.int32, (NCORR, chains), 0)
    ).astype(jnp.float32)
    selector = lax.dot_general(
        target_hits.astype(jnp.bfloat16),
        hits.astype(jnp.bfloat16),
        (((1,), (1,)), ((), ())),
        preferred_element_type=jnp.float32,
    )
    flag = live[0].astype(jnp.float32)

    token_wait(1)
    token_send(2)
    from_ring(0, first, far_y, 0)
    from_ring(0, second, far_y, 0)
    for half in range(2):
        arrived(sbuf.at[:, :, rows_of(half), :], sink_recv.at[half])

    tall = 2 * rows
    lhs_real = sbuf[:, 0].reshape(NF * tall, nop * rows)
    lhs_imag = sbuf[:, 1].reshape(NF * tall, nop * rows)
    left = lax.broadcasted_iota(jnp.int32, (NF * tall, 128), 1) < 64

    def mul(a, b):
        return jnp.dot(a, b, preferred_element_type=jnp.float32)

    def multiply(b):
        for n in range(2):
            low, high = slice(n * 128, n * 128 + 128), slice(n * 128 + 256, n * 128 + 384)
            right_real = jnp.concatenate([rfull[b, 0, :, low], rfull[b, 0, :, high]], axis=-1)
            right_imag = jnp.concatenate([rfull[b, 1, :, low], rfull[b, 1, :, high]], axis=-1)
            real = mul(lhs_real, right_real) - mul(lhs_imag, right_imag)
            imag = mul(lhs_real, right_imag) + mul(lhs_imag, right_real)
            for part, value in enumerate((real, imag)):
                one, two = value[:, :128], value[:, 128:]
                even = jnp.where(left, one, pltpu.roll(two, 64, 1)).astype(jnp.bfloat16)
                odd = jnp.where(left, pltpu.roll(one, 64, 1), two).astype(jnp.bfloat16)
                prod[2 * n, b, part] = even.reshape(NF, tall, 128)
                prod[2 * n + 1, b, part] = odd.reshape(NF, tall, 128)

    blocks = []
    far_blocks = []

    def give(b):
        near_copy = send(
            prod.at[taker_y, b],
            recv.at[1, b],
            block_send.at[b],
            block_recv.at[b],
            device(z, x, core, taker_y),
        )
        far_copy = send(
            prod.at[far_y, b],
            recv.at[2, b],
            block_send.at[2 + b],
            block_recv.at[2 + b],
            device(z, x, core, far_y),
        )

        @pl.when(gives_far)
        def _():
            far_copy.start()

        near_copy.start()
        blocks.append(near_copy)
        far_blocks.append(far_copy)

    def shared(b):
        for half in range(2):
            for y_at in range(ny):
                index = b * nop + half * ny + y_at
                arrived(chunk(b, 1 - core, half, y_at), pair_recv.at[index])

    shared(0)
    multiply(0)
    from_ring(1, first, right_y, 0)
    from_ring(1, second, left_y, 0)
    give(0)
    from_ring(1, first, far_y, 0)
    from_ring(1, second, far_y, 0)
    shared(1)
    multiply(1)
    recv[0] = prod[y] * jnp.bfloat16(0.5)
    give(1)
    token_wait(2)
    token_send(3)

    order = [(part, b, a) for part in range(2) for b in range(NF) for a in range(NF)]
    own = jnp.concatenate(
        [
            jnp.concatenate([prod[at_y, b, part, a] for part, b, a in order], axis=0)
            for at_y in (y, giver_y, far_y)
        ],
        axis=1,
    )
    place_row = lax.broadcasted_iota(jnp.int32, (8, 128), 0)
    place_lane = lax.broadcasted_iota(jnp.int32, (8, 128), 1)
    diagonal = lax.broadcasted_iota(jnp.int32, (tall, 256), 0) == lax.rem(
        lax.broadcasted_iota(jnp.int32, (tall, 256), 1), 128
    )
    total = jnp.zeros((8, 128), jnp.float32)
    for d in range(NF):
        blocks[d].wait_recv()

        @pl.when(jnp.logical_not(gives_far))
        def _(d=d):
            far_blocks[d].wait_recv()

        for c in range(NF):
            right = jnp.concatenate(
                [
                    jnp.concatenate([recv[slot, d, 0, c], recv[slot, d, 1, c]], axis=1)
                    for slot in range(3)
                ],
                axis=0,
            )
            square = mul(own, right).reshape(8, tall, 256)
            kept = jnp.where(diagonal, square, 0.0).sum(axis=1)
            with_real, with_imag = kept[:, :128], kept[:, 128:]
            real = with_real[:4] - with_imag[4:]
            imag = with_imag[:4] + with_real[4:]
            value = jnp.concatenate([real, imag], axis=0).sum(axis=1, keepdims=True)
            slot_at = place_lane == place_row * 8 + (core * 4 + d * 2 + c)
            total = total + jnp.where(slot_at, value, 0.0)
    lane = lax.broadcasted_iota(jnp.int32, (1, 128), 1)
    row_plane[...] = total.sum(axis=0, keepdims=True) + jnp.where(
        lane == 64 + here, flag * (1.0 / nop), 0.0
    )

    def exchange(buffer, me, source, peers, index):
        buffer[me] = source[...]
        for where in peers:
            send(source, buffer.at[me], red_send.at[index], red_recv.at[index], where).start()

    def exchanged(buffer, peers, index):
        arrived(buffer.at[pl.ds(0, len(peers))], red_recv.at[index])

    def around(d, n):
        return min(d, n - d)

    spots = [(dx, dy, k) for dx in range(NX) for dy in range(ny) for k in range(2)][1:]
    spots.sort(key=lambda s: -(around(s[0], NX) + around(s[1], ny)))
    exchange(
        plane,
        x * nop + core * ny + y,
        row_plane,
        [device(z, at(x, dx, NX), at(core, k, 2), at(y, dy, ny)) for dx, dy, k in spots],
        0,
    )
    exchanged(plane, spots, 0)
    sums = [plane[j * nop : (j + 1) * nop].sum(axis=0) for j in range(NX)]
    flags = sums[0] + sums[1] + sums[2] + sums[3]
    weighted = jnp.zeros((1, 128), jnp.float32)
    for j in range(NX):
        alive = jnp.where(lane == 64 + j, flags, 0.0).sum(axis=1, keepdims=True)
        weighted = weighted + alive * sums[j]
    row_z[...] = weighted

    token_wait(3)
    hops = sorted(range(1, nz), key=lambda d: -around(d, nz))
    exchange(line, z, row_z, [device(at(z, d, nz), x, core, y) for d in hops], 1)

    for copy, mine in outgoing:

        @pl.when(jnp.logical_not(mine))
        def _(copy=copy):
            copy.wait_send()

    for copy in ring + pairs + blocks:
        copy.wait_send()

    @pl.when(gives_far)
    def _():
        for copy in far_blocks:
            copy.wait_send()

    exchanged(line, hops, 1)
    everything = line[...].sum(axis=0)

    pick_row = lax.broadcasted_iota(jnp.int32, (8, 128), 0)
    pick_lane = lax.broadcasted_iota(jnp.int32, (8, 128), 1)
    picked = (pick_lane // 32 == pick_row // 2) & (
        lax.rem(pick_lane // 4, 2) == lax.rem(pick_row, 2)
    )
    spread = jnp.where(picked, everything * (1.0 / math.sqrt(ntm)), 0.0)
    result = lax.dot_general(
        spread,
        selector,
        (((1,), (1,)), ((), ())),
        precision=lax.Precision.HIGHEST,
        preferred_element_type=jnp.float32,
    )
    out_ref[...] = result[:4]

    arrived(plane.at[pl.ds(0, len(spots))], red_send.at[0])
    arrived(line.at[pl.ds(0, len(hops))], red_send.at[1])


def per_device(ntm, nop, sink, source, live, factors, target):
    rows, width = sink.shape[3], sink.shape[4]
    chains = target.shape[0]
    hbm = pl.BlockSpec(memory_space=pltpu.HBM)
    dma = pltpu.SemaphoreType.DMA
    pin = functools.partial(pltpu.with_memory_space_constraint, memory_space=pltpu.HBM)
    out = pl.pallas_call(
        functools.partial(kernel, ntm, nop),
        out_shape=jax.ShapeDtypeStruct((2 * WIN, NCORR), jnp.float32),
        in_specs=[hbm, hbm, pl.BlockSpec(memory_space=pltpu.SMEM), hbm, hbm],
        out_specs=pl.BlockSpec(memory_space=pltpu.VMEM),
        scratch_shapes=[
            pltpu.VMEM((NF, 2, width, width), jnp.bfloat16),
            pltpu.VMEM((NF, 2, 2 * rows, width), jnp.bfloat16),
            pltpu.VMEM((nop // 2, NF, 2, NF, 2 * rows, 128), jnp.bfloat16),
            pltpu.VMEM((3, NF, 2, NF, 2 * rows, 128), jnp.bfloat16),
            pltpu.VMEM((1, 128), jnp.float32),
            pltpu.VMEM((1, 128), jnp.float32),
            pltpu.VMEM((NX * nop, 1, 128), jnp.float32),
            pltpu.VMEM((ntm // NX, 1, 128), jnp.float32),
            pltpu.VMEM((4, chains), jnp.int32),
            pltpu.VMEM((1, chains), jnp.int32),
            dma((2,)),
            dma((2 * NF,)),
            dma((2 * NF,)),
            dma((WIN,)),
            dma((2,)),
            dma((6 * NF,)),
            dma((nop * NF,)),
            dma((nop * NF,)),
            dma((nop * NF,)),
            dma((4,)),
            dma((4,)),
            dma((2,)),
            dma((2,)),
            pltpu.SemaphoreType.REGULAR((8,)),
        ],
        compiler_params=pltpu.CompilerParams(
            collective_id=0, has_side_effects=True, vmem_limit_bytes=48 << 20
        ),
        name="correlate",
    )(pin(sink), pin(source), live, pin(factors.T), pin(target.reshape(1, chains)))
    return jnp.moveaxis(out.reshape(2, WIN, NCORR), 1, 2)


def solution(mesh):
    ntm, nop = mesh.shape["tm"], mesh.shape["op"]
    return jax.shard_map(
        functools.partial(per_device, ntm, nop),
        mesh=mesh,
        in_specs=(
            P("tm", None, None, "op", None),
            P("tm", None, None, "op", None),
            P("tm"),
            P(),
            P(),
        ),
        out_specs=P(),
        check_vma=False,
    )
```

```python
import functools
import math

import jax
import jax.numpy as jnp
from jax import lax
from jax.experimental import pallas as pl
from jax.experimental.pallas import tpu as pltpu
from jax.sharding import PartitionSpec as P

WIN = 2
NF = 2
NCORR = 16
NX = 4
MESH = pl.DeviceIdType.MESH


def kernel(
    ntm,
    nop,
    sink_hbm,
    source_hbm,
    live,
    factors_hbm,
    target_hbm,
    out_ref,
    rfull,
    sbuf,
    prod,
    recv,
    row_plane,
    row_z,
    plane,
    line,
    factors,
    target,
    local_sem,
    source_send,
    source_recv,
    sink_send,
    sink_recv,
    ring_send,
    ring_recv,
    pair_send,
    pair_recv,
    block_send,
    block_recv,
    red_send,
    red_recv,
    token,
):
    nz, ny = ntm // NX, nop // 2
    rows = source_hbm.shape[3]
    tm, op = lax.axis_index("tm"), lax.axis_index("op")
    z, hi = tm // NX, op // ny
    lo, core = lax.rem(tm // 2, 2), lax.rem(tm, 2)
    x, y = hi * 2 + lo, lax.rem(op, ny)
    here = lo * 2 + core

    def at(base, offset, count):
        return lax.rem(base + (offset % count), count)

    def device(z_at, x_at, core_at, y_at):
        return (z_at * NX + lax.rem(x_at, 2) * 2 + core_at, x_at // 2 * ny + y_at)

    def send(src, dst, send_sem, recv_sem, where):
        return pltpu.make_async_remote_copy(
            src_ref=src,
            dst_ref=dst,
            send_sem=send_sem,
            recv_sem=recv_sem,
            device_id=where,
            device_id_type=MESH,
        )

    def arrived(ref, sem):
        pltpu.make_async_copy(ref, ref, sem).wait()

    barrier = pltpu.get_barrier_semaphore()

    def greet(where):
        pl.semaphore_signal(barrier, inc=1, device_id=where, device_id_type=MESH)

    shifts = []
    greeted = 2 * NX - 1 + 2 * (ny - 1) + 2
    for w in range(WIN):
        back = here - (w + 1)
        wrap = (back < 0).astype(jnp.int32)
        column = back + wrap * NX
        where = device(lax.rem(z + nz - wrap, nz), column, w, y)
        shifts.append((where, (wrap == 0) & (column == x) & (core == w)))
        greeted = greeted + wrap

        @pl.when(wrap == 1)
        def _(where=where):
            greet(where)

    sink_time = x + core + 1
    greeted = greeted + jnp.where(sink_time >= NX, 2, 0)

    @pl.when(sink_time >= NX)
    def _():
        for half in range(2):
            greet((at(z, 1, nz) * NX + sink_time - NX, half * ny + y))

    spot = x * 2 + core
    for k in range(1, 2 * NX):
        other = at(spot, k, 2 * NX)
        greet(device(z, other // 2, lax.rem(other, 2), y))
    for dy in range(1, ny):
        for k in range(2):
            greet(device(z, x, at(core, k, 2), at(y, dy, ny)))
    for dz in (1, -1):
        greet(device(at(z, dz, nz), x, core, y))

    local = [
        pltpu.make_async_copy(factors_hbm, factors, local_sem.at[0]),
        pltpu.make_async_copy(target_hbm, target, local_sem.at[1]),
    ]
    for copy in local:
        copy.start()

    pl.semaphore_wait(barrier, greeted)

    def rows_of(index):
        return pl.ds(pl.multiple_of(index * rows, rows), rows)

    outgoing = []

    def launch(src, dst, send_sem, recv_sem, where, mine):
        copy = send(src, dst, send_sem, recv_sem, where)

        @pl.when(mine)
        def _():
            pltpu.make_async_copy(src, dst, recv_sem).start()

        @pl.when(jnp.logical_not(mine))
        def _():
            copy.start()

        outgoing.append((copy, mine))

    for b in range(NF):
        for part in range(2):
            launch(
                source_hbm.at[0, b, part],
                rfull.at[b, part, rows_of(op), :],
                source_send.at[b * 2 + part],
                source_recv.at[b * 2 + hi],
                device(z, here, part, y),
                (here == x) & (core == part),
            )
    ring = []
    pairs = []
    left_y, right_y, far_y = at(y, -1, ny), at(y, 1, ny), at(y, 2, ny)

    def chunk(b, part, half, y_at):
        return rfull.at[b, part, rows_of(half * ny + y_at), :]

    def pass_on(b, half, y_at, way):
        ref = chunk(b, core, half, y_at)
        copy = send(
            ref,
            ref,
            ring_send.at[len(ring)],
            ring_recv.at[b * nop + half * ny + y_at],
            device(z, x, core, at(y, way, ny)),
        )
        copy.start()
        ring.append(copy)

    def share(b, half, y_at):
        ref = chunk(b, core, half, y_at)
        index = b * nop + half * ny + y_at
        copy = send(
            ref,
            ref,
            pair_send.at[index],
            pair_recv.at[index],
            device(z, x, 1 - core, y),
        )
        copy.start()
        pairs.append(copy)

    step_y = 1 - 2 * core
    giver_y = lax.rem(y + step_y + ny, ny)
    taker_y = lax.rem(y - step_y + ny, ny)
    gives_far = lax.rem(y // 2 + core, 2) == 1
    tokens = []
    known = 1
    while known < nz // 2:
        tokens.append(known)
        known *= 2

    def token_send(step):
        if step < len(tokens):
            for way in (1, -1):
                where = device(at(z, way * tokens[step], nz), x, core, y)
                pl.semaphore_signal(token.at[step], inc=1, device_id=where, device_id_type=MESH)

    def token_wait(step):
        if step < len(tokens):
            pl.semaphore_wait(token.at[step], 2)

    token_send(0)
    first, second = hi, 1 - hi

    def from_source(b, half, way):
        arrived(chunk(b, core, half, y), source_recv.at[b * 2 + half])
        pass_on(b, half, y, way)
        pass_on(b, half, y, -way)
        share(b, half, y)

    def from_ring(b, half, y_at, way):
        arrived(chunk(b, core, half, y_at), ring_recv.at[b * nop + half * ny + y_at])
        if way:
            pass_on(b, half, y_at, way)
        share(b, half, y_at)

    from_source(0, first, 1)
    from_source(0, second, -1)
    for w, (where, mine) in enumerate(shifts):
        launch(
            sink_hbm.at[0],
            sbuf.at[:, :, rows_of(hi), :],
            sink_send.at[w],
            sink_recv.at[hi],
            where,
            mine,
        )

    from_source(1, first, 1)
    from_ring(0, first, left_y, 1)
    from_ring(0, second, right_y, -1)
    from_source(1, second, -1)
    token_wait(0)
    token_send(1)
    from_ring(0, first, right_y, 0)
    from_ring(0, second, left_y, 0)
    from_ring(1, first, left_y, 1)
    from_ring(1, second, right_y, -1)

    @pl.when(gives_far)
    def _():
        recv[2] = jnp.zeros(recv.shape[1:], recv.dtype)

    for copy in local:
        copy.wait()
    fac = factors[...]
    codes = fac[1:2] * 8 + fac[0:1] * 4 + fac[3:4] * 2 + fac[2:3]
    swapped = fac[3:4] * 8 + fac[2:3] * 4 + fac[1:2] * 2 + fac[0:1]
    chains = codes.shape[1]
    lane_row = lax.broadcasted_iota(jnp.int32, (128, chains), 0)
    lane_code = lax.rem(lane_row // 8, 4) * 4 + lax.rem(lane_row, 4)
    hits = (codes == lane_code).astype(jnp.float32) + (swapped == lane_code).astype(jnp.float32)
    target_hits = (
        target[...] == lax.broadcasted_iota(jnp.int32, (NCORR, chains), 0)
    ).astype(jnp.float32)
    selector = lax.dot_general(
        target_hits.astype(jnp.bfloat16),
        hits.astype(jnp.bfloat16),
        (((1,), (1,)), ((), ())),
        preferred_element_type=jnp.float32,
    )
    flag = live[0].astype(jnp.float32)

    token_wait(1)
    token_send(2)
    from_ring(0, first, far_y, 0)
    from_ring(0, second, far_y, 0)
    for half in range(2):
        arrived(sbuf.at[:, :, rows_of(half), :], sink_recv.at[half])

    tall = 2 * rows
    lhs_real = sbuf[:, 0].reshape(NF * tall, nop * rows)
    lhs_imag = sbuf[:, 1].reshape(NF * tall, nop * rows)
    left = lax.broadcasted_iota(jnp.int32, (NF * tall, 128), 1) < 64

    def mul(a, b):
        return jnp.dot(a, b, preferred_element_type=jnp.float32)

    def multiply(b):
        for n in range(2):
            low, high = slice(n * 128, n * 128 + 128), slice(n * 128 + 256, n * 128 + 384)
            right_real = jnp.concatenate([rfull[b, 0, :, low], rfull[b, 0, :, high]], axis=-1)
            right_imag = jnp.concatenate([rfull[b, 1, :, low], rfull[b, 1, :, high]], axis=-1)
            real = mul(lhs_real, right_real) - mul(lhs_imag, right_imag)
            imag = mul(lhs_real, right_imag) + mul(lhs_imag, right_real)
            for part, value in enumerate((real, imag)):
                one, two = value[:, :128], value[:, 128:]
                even = jnp.where(left, one, pltpu.roll(two, 64, 1)).astype(jnp.bfloat16)
                odd = jnp.where(left, pltpu.roll(one, 64, 1), two).astype(jnp.bfloat16)
                prod[2 * n, b, part] = even.reshape(NF, tall, 128)
                prod[2 * n + 1, b, part] = odd.reshape(NF, tall, 128)

    blocks = []
    far_blocks = []

    def give(b):
        near_copy = send(
            prod.at[taker_y, b],
            recv.at[1, b],
            block_send.at[b],
            block_recv.at[b],
            device(z, x, core, taker_y),
        )
        far_copy = send(
            prod.at[far_y, b],
            recv.at[2, b],
            block_send.at[2 + b],
            block_recv.at[2 + b],
            device(z, x, core, far_y),
        )

        @pl.when(gives_far)
        def _():
            far_copy.start()

        near_copy.start()
        blocks.append(near_copy)
        far_blocks.append(far_copy)

    def shared(b):
        for half in range(2):
            for y_at in range(ny):
                index = b * nop + half * ny + y_at
                arrived(chunk(b, 1 - core, half, y_at), pair_recv.at[index])

    shared(0)
    multiply(0)
    from_ring(1, first, right_y, 0)
    from_ring(1, second, left_y, 0)
    give(0)
    from_ring(1, first, far_y, 0)
    from_ring(1, second, far_y, 0)
    shared(1)
    multiply(1)
    recv[0] = prod[y] * jnp.bfloat16(0.5)
    give(1)
    token_wait(2)
    token_send(3)

    order = [(part, b, a) for part in range(2) for b in range(NF) for a in range(NF)]
    own = jnp.concatenate(
        [
            jnp.concatenate([prod[at_y, b, part, a] for part, b, a in order], axis=0)
            for at_y in (y, giver_y, far_y)
        ],
        axis=1,
    )
    place_row = lax.broadcasted_iota(jnp.int32, (8, 128), 0)
    place_lane = lax.broadcasted_iota(jnp.int32, (8, 128), 1)
    diagonal = lax.broadcasted_iota(jnp.int32, (tall, 256), 0) == lax.rem(
        lax.broadcasted_iota(jnp.int32, (tall, 256), 1), 128
    )
    total = jnp.zeros((8, 128), jnp.float32)
    for d in range(NF):
        blocks[d].wait_recv()

        @pl.when(jnp.logical_not(gives_far))
        def _(d=d):
            far_blocks[d].wait_recv()

        for c in range(NF):
            right = jnp.concatenate(
                [
                    jnp.concatenate([recv[slot, d, 0, c], recv[slot, d, 1, c]], axis=1)
                    for slot in range(3)
                ],
                axis=0,
            )
            square = mul(own, right).reshape(8, tall, 256)
            kept = jnp.where(diagonal, square, 0.0).sum(axis=1)
            with_real, with_imag = kept[:, :128], kept[:, 128:]
            real = with_real[:4] - with_imag[4:]
            imag = with_imag[:4] + with_real[4:]
            value = jnp.concatenate([real, imag], axis=0).sum(axis=1, keepdims=True)
            slot_at = place_lane == place_row * 8 + (core * 4 + d * 2 + c)
            total = total + jnp.where(slot_at, value, 0.0)
    lane = lax.broadcasted_iota(jnp.int32, (1, 128), 1)
    row_plane[...] = total.sum(axis=0, keepdims=True) + jnp.where(
        lane == 64 + here, flag * (1.0 / nop), 0.0
    )

    def exchange(buffer, me, source, peers, index):
        buffer[me] = source[...]
        for where in peers:
            send(source, buffer.at[me], red_send.at[index], red_recv.at[index], where).start()

    def exchanged(buffer, peers, index):
        arrived(buffer.at[pl.ds(0, len(peers))], red_recv.at[index])

    def around(d, n):
        return min(d, n - d)

    spots = [(dx, dy, k) for dx in range(NX) for dy in range(ny) for k in range(2)][1:]
    spots.sort(key=lambda s: -(around(s[0], NX) + around(s[1], ny)))
    exchange(
        plane,
        x * nop + core * ny + y,
        row_plane,
        [device(z, at(x, dx, NX), at(core, k, 2), at(y, dy, ny)) for dx, dy, k in spots],
        0,
    )
    exchanged(plane, spots, 0)
    sums = [plane[j * nop : (j + 1) * nop].sum(axis=0) for j in range(NX)]
    flags = sums[0] + sums[1] + sums[2] + sums[3]
    weighted = jnp.zeros((1, 128), jnp.float32)
    for j in range(NX):
        alive = jnp.where(lane == 64 + j, flags, 0.0).sum(axis=1, keepdims=True)
        weighted = weighted + alive * sums[j]
    row_z[...] = weighted

    token_wait(3)
    hops = sorted(range(1, nz), key=lambda d: -around(d, nz))
    exchange(line, z, row_z, [device(at(z, d, nz), x, core, y) for d in hops], 1)

    for copy, mine in outgoing:

        @pl.when(jnp.logical_not(mine))
        def _(copy=copy):
            copy.wait_send()

    for copy in ring + pairs + blocks:
        copy.wait_send()

    @pl.when(gives_far)
    def _():
        for copy in far_blocks:
            copy.wait_send()

    exchanged(line, hops, 1)
    everything = line[...].sum(axis=0)

    pick_row = lax.broadcasted_iota(jnp.int32, (8, 128), 0)
    pick_lane = lax.broadcasted_iota(jnp.int32, (8, 128), 1)
    picked = (pick_lane // 32 == pick_row // 2) & (
        lax.rem(pick_lane // 4, 2) == lax.rem(pick_row, 2)
    )
    spread = jnp.where(picked, everything * (1.0 / math.sqrt(ntm)), 0.0)
    result = lax.dot_general(
        spread,
        selector,
        (((1,), (1,)), ((), ())),
        precision=lax.Precision.HIGHEST,
        preferred_element_type=jnp.float32,
    )
    out_ref[...] = result[:4]

    arrived(plane.at[pl.ds(0, len(spots))], red_send.at[0])
    arrived(line.at[pl.ds(0, len(hops))], red_send.at[1])


def per_device(ntm, nop, sink, source, live, factors, target):
    rows, width = sink.shape[3], sink.shape[4]
    chains = target.shape[0]
    hbm = pl.BlockSpec(memory_space=pltpu.HBM)
    dma = pltpu.SemaphoreType.DMA
    pin = functools.partial(pltpu.with_memory_space_constraint, memory_space=pltpu.HBM)
    out = pl.pallas_call(
        functools.partial(kernel, ntm, nop),
        out_shape=jax.ShapeDtypeStruct((2 * WIN, NCORR), jnp.float32),
        in_specs=[hbm, hbm, pl.BlockSpec(memory_space=pltpu.SMEM), hbm, hbm],
        out_specs=pl.BlockSpec(memory_space=pltpu.VMEM),
        scratch_shapes=[
            pltpu.VMEM((NF, 2, width, width), jnp.bfloat16),
            pltpu.VMEM((NF, 2, 2 * rows, width), jnp.bfloat16),
            pltpu.VMEM((nop // 2, NF, 2, NF, 2 * rows, 128), jnp.bfloat16),
            pltpu.VMEM((3, NF, 2, NF, 2 * rows, 128), jnp.bfloat16),
            pltpu.VMEM((1, 128), jnp.float32),
            pltpu.VMEM((1, 128), jnp.float32),
            pltpu.VMEM((NX * nop, 1, 128), jnp.float32),
            pltpu.VMEM((ntm // NX, 1, 128), jnp.float32),
            pltpu.VMEM((4, chains), jnp.int32),
            pltpu.VMEM((1, chains), jnp.int32),
            dma((2,)),
            dma((2 * NF,)),
            dma((2 * NF,)),
            dma((WIN,)),
            dma((2,)),
            dma((6 * NF,)),
            dma((nop * NF,)),
            dma((nop * NF,)),
            dma((nop * NF,)),
            dma((4,)),
            dma((4,)),
            dma((2,)),
            dma((2,)),
            pltpu.SemaphoreType.REGULAR((8,)),
        ],
        compiler_params=pltpu.CompilerParams(
            collective_id=0, has_side_effects=True, vmem_limit_bytes=48 << 20
        ),
        name="correlate",
    )(pin(sink), pin(source), live, pin(factors.T), pin(target.reshape(1, chains)))
    return jnp.moveaxis(out.reshape(2, WIN, NCORR), 1, 2)


def solution(mesh):
    ntm, nop = mesh.shape["tm"], mesh.shape["op"]
    return jax.shard_map(
        functools.partial(per_device, ntm, nop),
        mesh=mesh,
        in_specs=(
            P("tm", None, None, "op", None),
            P("tm", None, None, "op", None),
            P("tm"),
            P(),
            P(),
        ),
        out_specs=P(),
        check_vma=False,
    )
```

```python
import functools
import math

import jax
import jax.numpy as jnp
from jax import lax
from jax.experimental import pallas as pl
from jax.experimental.pallas import tpu as pltpu
from jax.sharding import PartitionSpec as P

WIN = 2
NF = 2
NCORR = 16
NX = 4
MESH = pl.DeviceIdType.MESH


def kernel(
    ntm,
    nop,
    sink_hbm,
    source_hbm,
    live,
    factors_hbm,
    target_hbm,
    out_ref,
    rfull,
    sbuf,
    prod,
    recv,
    row_plane,
    row_z,
    plane,
    line,
    factors,
    target,
    local_sem,
    source_send,
    source_recv,
    sink_send,
    sink_recv,
    ring_send,
    ring_recv,
    pair_send,
    pair_recv,
    block_send,
    block_recv,
    red_send,
    red_recv,
    token,
):
    nz, ny = ntm // NX, nop // 2
    rows = source_hbm.shape[3]
    tm, op = lax.axis_index("tm"), lax.axis_index("op")
    z, hi = tm // NX, op // ny
    lo, core = lax.rem(tm // 2, 2), lax.rem(tm, 2)
    x, y = hi * 2 + lo, lax.rem(op, ny)
    here = lo * 2 + core

    def column_of(j):
        return lax.rem(2 * j + 1, 5)

    mine_j = lax.rem(3 * x + 2, 5)

    def at(base, offset, count):
        return lax.rem(base + (offset % count), count)

    def device(z_at, x_at, core_at, y_at):
        return (z_at * NX + lax.rem(x_at, 2) * 2 + core_at, x_at // 2 * ny + y_at)

    def send(src, dst, send_sem, recv_sem, where):
        return pltpu.make_async_remote_copy(
            src_ref=src,
            dst_ref=dst,
            send_sem=send_sem,
            recv_sem=recv_sem,
            device_id=where,
            device_id_type=MESH,
        )

    def arrived(ref, sem):
        pltpu.make_async_copy(ref, ref, sem).wait()

    barrier = pltpu.get_barrier_semaphore()

    def greet(where):
        pl.semaphore_signal(barrier, inc=1, device_id=where, device_id_type=MESH)

    shifts = []
    greeted = 2 * NX - 1 + 2 * (ny - 1) + 2
    for w in range(WIN):
        back = here - (w + 1)
        wrap = (back < 0).astype(jnp.int32)
        column = column_of(back + wrap * NX)
        where = device(lax.rem(z + nz - wrap, nz), column, w, y)
        shifts.append((where, (wrap == 0) & (column == x) & (core == w)))
        greeted = greeted + wrap

        @pl.when(wrap == 1)
        def _(where=where):
            greet(where)

    sink_time = mine_j + core + 1
    greeted = greeted + jnp.where(sink_time >= NX, 2, 0)

    @pl.when(sink_time >= NX)
    def _():
        for half in range(2):
            greet((at(z, 1, nz) * NX + sink_time - NX, half * ny + y))

    spot = x * 2 + core
    for k in range(1, 2 * NX):
        other = at(spot, k, 2 * NX)
        greet(device(z, other // 2, lax.rem(other, 2), y))
    for dy in range(1, ny):
        for k in range(2):
            greet(device(z, x, at(core, k, 2), at(y, dy, ny)))
    for dz in (1, -1):
        greet(device(at(z, dz, nz), x, core, y))

    local = [
        pltpu.make_async_copy(factors_hbm, factors, local_sem.at[0]),
        pltpu.make_async_copy(target_hbm, target, local_sem.at[1]),
    ]
    for copy in local:
        copy.start()

    pl.semaphore_wait(barrier, greeted)

    def rows_of(index):
        return pl.ds(pl.multiple_of(index * rows, rows), rows)

    outgoing = []

    def launch(src, dst, send_sem, recv_sem, where, mine):
        copy = send(src, dst, send_sem, recv_sem, where)

        @pl.when(mine)
        def _():
            pltpu.make_async_copy(src, dst, recv_sem).start()

        @pl.when(jnp.logical_not(mine))
        def _():
            copy.start()

        outgoing.append((copy, mine))

    for b in range(NF):
        for part in range(2):
            launch(
                source_hbm.at[0, b, part],
                rfull.at[b, part, rows_of(op), :],
                source_send.at[b * 2 + part],
                source_recv.at[b * 2 + hi],
                device(z, column_of(here), part, y),
                (column_of(here) == x) & (core == part),
            )
    ring = []
    pairs = []
    left_y, right_y, far_y = at(y, -1, ny), at(y, 1, ny), at(y, 2, ny)

    def chunk(b, part, half, y_at):
        return rfull.at[b, part, rows_of(half * ny + y_at), :]

    def pass_on(b, half, y_at, way):
        ref = chunk(b, core, half, y_at)
        copy = send(
            ref,
            ref,
            ring_send.at[len(ring)],
            ring_recv.at[b * nop + half * ny + y_at],
            device(z, x, core, at(y, way, ny)),
        )
        copy.start()
        ring.append(copy)

    def share(b, half, y_at):
        ref = chunk(b, core, half, y_at)
        index = b * nop + half * ny + y_at
        copy = send(
            ref,
            ref,
            pair_send.at[index],
            pair_recv.at[index],
            device(z, x, 1 - core, y),
        )
        copy.start()
        pairs.append(copy)

    step_y = 1 - 2 * core
    giver_y = lax.rem(y + step_y + ny, ny)
    taker_y = lax.rem(y - step_y + ny, ny)
    gives_far = lax.rem(y // 2 + core, 2) == 1
    tokens = []
    known = 1
    while known < nz // 2:
        tokens.append(known)
        known *= 2

    def token_send(step):
        if step < len(tokens):
            for way in (1, -1):
                where = device(at(z, way * tokens[step], nz), x, core, y)
                pl.semaphore_signal(token.at[step], inc=1, device_id=where, device_id_type=MESH)

    def token_wait(step):
        if step < len(tokens):
            pl.semaphore_wait(token.at[step], 2)

    token_send(0)
    first, second = hi, 1 - hi

    def from_source(b, half, way):
        arrived(chunk(b, core, half, y), source_recv.at[b * 2 + half])
        pass_on(b, half, y, way)
        pass_on(b, half, y, -way)
        share(b, half, y)

    def from_ring(b, half, y_at, way):
        arrived(chunk(b, core, half, y_at), ring_recv.at[b * nop + half * ny + y_at])
        if way:
            pass_on(b, half, y_at, way)
        share(b, half, y_at)

    from_source(0, first, 1)
    from_source(0, second, -1)
    for w, (where, mine) in enumerate(shifts):
        launch(
            sink_hbm.at[0],
            sbuf.at[:, :, rows_of(hi), :],
            sink_send.at[w],
            sink_recv.at[hi],
            where,
            mine,
        )

    from_source(1, first, 1)
    from_ring(0, first, left_y, 1)
    from_ring(0, second, right_y, -1)
    from_source(1, second, -1)
    token_wait(0)
    token_send(1)
    from_ring(0, first, right_y, 0)
    from_ring(0, second, left_y, 0)
    from_ring(1, first, left_y, 1)
    from_ring(1, second, right_y, -1)

    @pl.when(gives_far)
    def _():
        recv[2] = jnp.zeros(recv.shape[1:], recv.dtype)

    for copy in local:
        copy.wait()
    fac = factors[...]
    codes = fac[1:2] * 8 + fac[0:1] * 4 + fac[3:4] * 2 + fac[2:3]
    swapped = fac[3:4] * 8 + fac[2:3] * 4 + fac[1:2] * 2 + fac[0:1]
    chains = codes.shape[1]
    lane_row = lax.broadcasted_iota(jnp.int32, (128, chains), 0)
    lane_code = lax.rem(lane_row // 8, 4) * 4 + lax.rem(lane_row, 4)
    hits = (codes == lane_code).astype(jnp.float32) + (swapped == lane_code).astype(jnp.float32)
    target_hits = (
        target[...] == lax.broadcasted_iota(jnp.int32, (NCORR, chains), 0)
    ).astype(jnp.float32)
    selector = lax.dot_general(
        target_hits.astype(jnp.bfloat16),
        hits.astype(jnp.bfloat16),
        (((1,), (1,)), ((), ())),
        preferred_element_type=jnp.float32,
    )
    flag = live[0].astype(jnp.float32)

    token_wait(1)
    token_send(2)
    from_ring(0, first, far_y, 0)
    from_ring(0, second, far_y, 0)
    for half in range(2):
        arrived(sbuf.at[:, :, rows_of(half), :], sink_recv.at[half])

    tall = 2 * rows
    lhs_real = sbuf[:, 0].reshape(NF * tall, nop * rows)
    lhs_imag = sbuf[:, 1].reshape(NF * tall, nop * rows)
    left = lax.broadcasted_iota(jnp.int32, (NF * tall, 128), 1) < 64

    def mul(a, b):
        return jnp.dot(a, b, preferred_element_type=jnp.float32)

    def multiply(b):
        for n in range(2):
            low, high = slice(n * 128, n * 128 + 128), slice(n * 128 + 256, n * 128 + 384)
            right_real = jnp.concatenate([rfull[b, 0, :, low], rfull[b, 0, :, high]], axis=-1)
            right_imag = jnp.concatenate([rfull[b, 1, :, low], rfull[b, 1, :, high]], axis=-1)
            real = mul(lhs_real, right_real) - mul(lhs_imag, right_imag)
            imag = mul(lhs_real, right_imag) + mul(lhs_imag, right_real)
            for part, value in enumerate((real, imag)):
                one, two = value[:, :128], value[:, 128:]
                even = jnp.where(left, one, pltpu.roll(two, 64, 1)).astype(jnp.bfloat16)
                odd = jnp.where(left, pltpu.roll(one, 64, 1), two).astype(jnp.bfloat16)
                prod[2 * n, b, part] = even.reshape(NF, tall, 128)
                prod[2 * n + 1, b, part] = odd.reshape(NF, tall, 128)

    blocks = []
    far_blocks = []

    def give(b):
        near_copy = send(
            prod.at[taker_y, b],
            recv.at[1, b],
            block_send.at[b],
            block_recv.at[b],
            device(z, x, core, taker_y),
        )
        far_copy = send(
            prod.at[far_y, b],
            recv.at[2, b],
            block_send.at[2 + b],
            block_recv.at[2 + b],
            device(z, x, core, far_y),
        )

        @pl.when(gives_far)
        def _():
            far_copy.start()

        near_copy.start()
        blocks.append(near_copy)
        far_blocks.append(far_copy)

    def shared(b):
        for half in range(2):
            for y_at in range(ny):
                index = b * nop + half * ny + y_at
                arrived(chunk(b, 1 - core, half, y_at), pair_recv.at[index])

    shared(0)
    multiply(0)
    from_ring(1, first, right_y, 0)
    from_ring(1, second, left_y, 0)
    give(0)
    from_ring(1, first, far_y, 0)
    from_ring(1, second, far_y, 0)
    shared(1)
    multiply(1)
    recv[0] = prod[y] * jnp.bfloat16(0.5)
    give(1)
    token_wait(2)
    token_send(3)

    order = [(part, b, a) for part in range(2) for b in range(NF) for a in range(NF)]
    own, near, far = [
        jnp.concatenate([prod[at_y, b, part, a] for part, b, a in order], axis=0)
        for at_y in (y, giver_y, far_y)
    ]
    others = jnp.concatenate([near, far], axis=1)
    place_row = lax.broadcasted_iota(jnp.int32, (8, 128), 0)
    place_lane = lax.broadcasted_iota(jnp.int32, (8, 128), 1)
    diagonal = lax.broadcasted_iota(jnp.int32, (tall, 256), 0) == lax.rem(
        lax.broadcasted_iota(jnp.int32, (tall, 256), 1), 128
    )
    total = jnp.zeros((8, 128), jnp.float32)

    def pair_of(slot, d, c):
        return jnp.concatenate([recv[slot, d, 0, c], recv[slot, d, 1, c]], axis=1)

    def traced(lhs, rhs):
        square = mul(lhs, rhs).reshape(8, tall, 256)
        return jnp.where(diagonal, square, 0.0).sum(axis=1)

    alone = [[traced(own, pair_of(0, d, c)) for c in range(NF)] for d in range(NF)]
    for d in range(NF):
        blocks[d].wait_recv()

        @pl.when(jnp.logical_not(gives_far))
        def _(d=d):
            far_blocks[d].wait_recv()

        for c in range(NF):
            right = jnp.concatenate([pair_of(1, d, c), pair_of(2, d, c)], axis=0)
            kept = alone[d][c] + traced(others, right)
            with_real, with_imag = kept[:, :128], kept[:, 128:]
            real = with_real[:4] - with_imag[4:]
            imag = with_imag[:4] + with_real[4:]
            value = jnp.concatenate([real, imag], axis=0).sum(axis=1, keepdims=True)
            slot_at = place_lane == place_row * 8 + (core * 4 + d * 2 + c)
            total = total + jnp.where(slot_at, value, 0.0)
    lane = lax.broadcasted_iota(jnp.int32, (1, 128), 1)
    row_plane[...] = total.sum(axis=0, keepdims=True) + jnp.where(
        lane == 64 + here, flag * (1.0 / nop), 0.0
    )

    def exchange(buffer, me, source, peers, index):
        buffer[me] = source[...]
        for where in peers:
            send(source, buffer.at[me], red_send.at[index], red_recv.at[index], where).start()

    def exchanged(buffer, peers, index):
        arrived(buffer.at[pl.ds(0, len(peers))], red_recv.at[index])

    def around(d, n):
        return min(d, n - d)

    spots = [(dx, dy, k) for dx in range(NX) for dy in range(ny) for k in range(2)][1:]
    spots.sort(key=lambda s: -(around(s[0], NX) + around(s[1], ny)))
    exchange(
        plane,
        x * nop + core * ny + y,
        row_plane,
        [device(z, at(x, dx, NX), at(core, k, 2), at(y, dy, ny)) for dx, dy, k in spots],
        0,
    )
    exchanged(plane, spots, 0)
    sums = [plane[j * nop : (j + 1) * nop].sum(axis=0) for j in range(NX)]
    flags = sums[0] + sums[1] + sums[2] + sums[3]
    weighted = jnp.zeros((1, 128), jnp.float32)
    for j in range(NX):
        alive = jnp.where(lane == 64 + (3 * j + 2) % 5, flags, 0.0).sum(axis=1, keepdims=True)
        weighted = weighted + alive * sums[j]
    row_z[...] = weighted

    token_wait(3)
    hops = sorted(range(1, nz), key=lambda d: -around(d, nz))
    exchange(line, z, row_z, [device(at(z, d, nz), x, core, y) for d in hops], 1)

    for copy, mine in outgoing:

        @pl.when(jnp.logical_not(mine))
        def _(copy=copy):
            copy.wait_send()

    for copy in ring + pairs + blocks:
        copy.wait_send()

    @pl.when(gives_far)
    def _():
        for copy in far_blocks:
            copy.wait_send()

    exchanged(line, hops, 1)
    everything = line[...].sum(axis=0)

    pick_row = lax.broadcasted_iota(jnp.int32, (8, 128), 0)
    pick_lane = lax.broadcasted_iota(jnp.int32, (8, 128), 1)
    picked = (pick_lane // 32 == pick_row // 2) & (
        lax.rem(pick_lane // 4, 2) == lax.rem(pick_row, 2)
    )
    spread = jnp.where(picked, everything * (1.0 / math.sqrt(ntm)), 0.0)
    result = lax.dot_general(
        spread,
        selector,
        (((1,), (1,)), ((), ())),
        precision=lax.Precision.HIGHEST,
        preferred_element_type=jnp.float32,
    )
    out_ref[...] = result[:4]

    arrived(plane.at[pl.ds(0, len(spots))], red_send.at[0])
    arrived(line.at[pl.ds(0, len(hops))], red_send.at[1])


def per_device(ntm, nop, sink, source, live, factors, target):
    rows, width = sink.shape[3], sink.shape[4]
    chains = target.shape[0]
    hbm = pl.BlockSpec(memory_space=pltpu.HBM)
    dma = pltpu.SemaphoreType.DMA
    pin = functools.partial(pltpu.with_memory_space_constraint, memory_space=pltpu.HBM)
    out = pl.pallas_call(
        functools.partial(kernel, ntm, nop),
        out_shape=jax.ShapeDtypeStruct((2 * WIN, NCORR), jnp.float32),
        in_specs=[hbm, hbm, pl.BlockSpec(memory_space=pltpu.SMEM), hbm, hbm],
        out_specs=pl.BlockSpec(memory_space=pltpu.VMEM),
        scratch_shapes=[
            pltpu.VMEM((NF, 2, width, width), jnp.bfloat16),
            pltpu.VMEM((NF, 2, 2 * rows, width), jnp.bfloat16),
            pltpu.VMEM((nop // 2, NF, 2, NF, 2 * rows, 128), jnp.bfloat16),
            pltpu.VMEM((3, NF, 2, NF, 2 * rows, 128), jnp.bfloat16),
            pltpu.VMEM((1, 128), jnp.float32),
            pltpu.VMEM((1, 128), jnp.float32),
            pltpu.VMEM((NX * nop, 1, 128), jnp.float32),
            pltpu.VMEM((ntm // NX, 1, 128), jnp.float32),
            pltpu.VMEM((4, chains), jnp.int32),
            pltpu.VMEM((1, chains), jnp.int32),
            dma((2,)),
            dma((2 * NF,)),
            dma((2 * NF,)),
            dma((WIN,)),
            dma((2,)),
            dma((6 * NF,)),
            dma((nop * NF,)),
            dma((nop * NF,)),
            dma((nop * NF,)),
            dma((4,)),
            dma((4,)),
            dma((2,)),
            dma((2,)),
            pltpu.SemaphoreType.REGULAR((8,)),
        ],
        compiler_params=pltpu.CompilerParams(
            collective_id=0, has_side_effects=True, vmem_limit_bytes=48 << 20
        ),
        name="correlate",
    )(pin(sink), pin(source), live, pin(factors.T), pin(target.reshape(1, chains)))
    return jnp.moveaxis(out.reshape(2, WIN, NCORR), 1, 2)


def solution(mesh):
    ntm, nop = mesh.shape["tm"], mesh.shape["op"]
    return jax.shard_map(
        functools.partial(per_device, ntm, nop),
        mesh=mesh,
        in_specs=(
            P("tm", None, None, "op", None),
            P("tm", None, None, "op", None),
            P("tm"),
            P(),
            P(),
        ),
        out_specs=P(),
        check_vma=False,
    )
```

```python
import functools
import math

import jax
import jax.numpy as jnp
from jax import lax
from jax.experimental import pallas as pl
from jax.experimental.pallas import tpu as pltpu
from jax.sharding import PartitionSpec as P

WIN = 2
NF = 2
NCORR = 16
NX = 4
MESH = pl.DeviceIdType.MESH


def kernel(
    ntm,
    nop,
    sink_hbm,
    source_hbm,
    live,
    factors_hbm,
    target_hbm,
    out_ref,
    rfull,
    sbuf,
    prod,
    recv,
    row_plane,
    row_z,
    plane,
    line,
    factors,
    target,
    local_sem,
    source_send,
    source_recv,
    sink_send,
    sink_recv,
    ring_send,
    ring_recv,
    pair_send,
    pair_recv,
    block_send,
    block_recv,
    red_send,
    red_recv,
    token,
):
    nz, ny = ntm // NX, nop // 2
    rows = source_hbm.shape[3]
    tm, op = lax.axis_index("tm"), lax.axis_index("op")
    z, hi = tm // NX, op // ny
    lo, core = lax.rem(tm // 2, 2), lax.rem(tm, 2)
    x, y = hi * 2 + lo, lax.rem(op, ny)
    here = lo * 2 + core

    def column_of(j):
        return lax.rem(2 * j + 1, 5)

    mine_j = lax.rem(3 * x + 2, 5)

    def at(base, offset, count):
        return lax.rem(base + (offset % count), count)

    def device(z_at, x_at, core_at, y_at):
        return (z_at * NX + lax.rem(x_at, 2) * 2 + core_at, x_at // 2 * ny + y_at)

    def send(src, dst, send_sem, recv_sem, where):
        return pltpu.make_async_remote_copy(
            src_ref=src,
            dst_ref=dst,
            send_sem=send_sem,
            recv_sem=recv_sem,
            device_id=where,
            device_id_type=MESH,
        )

    def arrived(ref, sem):
        pltpu.make_async_copy(ref, ref, sem).wait()

    barrier = pltpu.get_barrier_semaphore()

    def greet(where):
        pl.semaphore_signal(barrier, inc=1, device_id=where, device_id_type=MESH)

    shifts = []
    greeted = 2 * NX - 1 + 2 * (ny - 1) + 2
    for w in range(WIN):
        back = here - (w + 1)
        wrap = (back < 0).astype(jnp.int32)
        column = column_of(back + wrap * NX)
        where = device(lax.rem(z + nz - wrap, nz), column, w, y)
        shifts.append((where, (wrap == 0) & (column == x) & (core == w)))
        greeted = greeted + wrap

        @pl.when(wrap == 1)
        def _(where=where):
            greet(where)

    sink_time = mine_j + core + 1
    greeted = greeted + jnp.where(sink_time >= NX, 2, 0)

    @pl.when(sink_time >= NX)
    def _():
        for half in range(2):
            greet((at(z, 1, nz) * NX + sink_time - NX, half * ny + y))

    spot = x * 2 + core
    for k in range(1, 2 * NX):
        other = at(spot, k, 2 * NX)
        greet(device(z, other // 2, lax.rem(other, 2), y))
    for dy in range(1, ny):
        for k in range(2):
            greet(device(z, x, at(core, k, 2), at(y, dy, ny)))
    for dz in (1, -1):
        greet(device(at(z, dz, nz), x, core, y))

    local = [
        pltpu.make_async_copy(factors_hbm, factors, local_sem.at[0]),
        pltpu.make_async_copy(target_hbm, target, local_sem.at[1]),
    ]
    for copy in local:
        copy.start()

    pl.semaphore_wait(barrier, greeted)

    def rows_of(index):
        return pl.ds(pl.multiple_of(index * rows, rows), rows)

    outgoing = []

    def launch(src, dst, send_sem, recv_sem, where, mine):
        copy = send(src, dst, send_sem, recv_sem, where)

        @pl.when(mine)
        def _():
            pltpu.make_async_copy(src, dst, recv_sem).start()

        @pl.when(jnp.logical_not(mine))
        def _():
            copy.start()

        outgoing.append((copy, mine))

    for b in range(NF):
        for part in range(2):
            launch(
                source_hbm.at[0, b, part],
                rfull.at[b, part, rows_of(op), :],
                source_send.at[b * 2 + part],
                source_recv.at[b * 2 + hi],
                device(z, column_of(here), part, y),
                (column_of(here) == x) & (core == part),
            )
    ring = []
    pairs = []
    left_y, right_y, far_y = at(y, -1, ny), at(y, 1, ny), at(y, 2, ny)

    def chunk(b, part, half, y_at):
        return rfull.at[b, part, rows_of(half * ny + y_at), :]

    def pass_on(b, half, y_at, way):
        ref = chunk(b, core, half, y_at)
        copy = send(
            ref,
            ref,
            ring_send.at[len(ring)],
            ring_recv.at[b * nop + half * ny + y_at],
            device(z, x, core, at(y, way, ny)),
        )
        copy.start()
        ring.append(copy)

    def share(b, half, y_at):
        ref = chunk(b, core, half, y_at)
        index = b * nop + half * ny + y_at
        copy = send(
            ref,
            ref,
            pair_send.at[index],
            pair_recv.at[index],
            device(z, x, 1 - core, y),
        )
        copy.start()
        pairs.append(copy)

    step_y = 1 - 2 * core
    giver_y = lax.rem(y + step_y + ny, ny)
    taker_y = lax.rem(y - step_y + ny, ny)
    gives_far = lax.rem(y // 2 + core, 2) == 1
    tokens = []
    known = 1
    while known < nz // 2:
        tokens.append(known)
        known *= 2

    def token_send(step):
        if step < len(tokens):
            for way in (1, -1):
                where = device(at(z, way * tokens[step], nz), x, core, y)
                pl.semaphore_signal(token.at[step], inc=1, device_id=where, device_id_type=MESH)

    def token_wait(step):
        if step < len(tokens):
            pl.semaphore_wait(token.at[step], 2)

    token_send(0)
    first, second = hi, 1 - hi

    def from_source(b, half, way):
        arrived(chunk(b, core, half, y), source_recv.at[b * 2 + half])
        pass_on(b, half, y, way)
        pass_on(b, half, y, -way)
        share(b, half, y)

    def from_ring(b, half, y_at, way):
        arrived(chunk(b, core, half, y_at), ring_recv.at[b * nop + half * ny + y_at])
        if way:
            pass_on(b, half, y_at, way)
        share(b, half, y_at)

    from_source(0, first, 1)
    from_source(0, second, -1)
    for w, (where, mine) in enumerate(shifts):
        launch(
            sink_hbm.at[0],
            sbuf.at[:, :, rows_of(hi), :],
            sink_send.at[w],
            sink_recv.at[hi],
            where,
            mine,
        )

    from_source(1, first, 1)
    from_source(1, second, -1)
    from_ring(0, first, left_y, 1)
    from_ring(0, second, right_y, -1)
    token_wait(0)
    token_send(1)
    from_ring(0, first, right_y, 0)
    from_ring(0, second, left_y, 0)
    from_ring(1, first, left_y, 1)
    from_ring(1, second, right_y, -1)

    @pl.when(gives_far)
    def _():
        recv[2] = jnp.zeros(recv.shape[1:], recv.dtype)

    for copy in local:
        copy.wait()
    fac = factors[...]
    codes = fac[1:2] * 8 + fac[0:1] * 4 + fac[3:4] * 2 + fac[2:3]
    swapped = fac[3:4] * 8 + fac[2:3] * 4 + fac[1:2] * 2 + fac[0:1]
    chains = codes.shape[1]
    lane_row = lax.broadcasted_iota(jnp.int32, (128, chains), 0)
    lane_code = lax.rem(lane_row // 8, 4) * 4 + lax.rem(lane_row, 4)
    hits = (codes == lane_code).astype(jnp.float32) + (swapped == lane_code).astype(jnp.float32)
    target_hits = (
        target[...] == lax.broadcasted_iota(jnp.int32, (NCORR, chains), 0)
    ).astype(jnp.float32)
    selector = lax.dot_general(
        target_hits.astype(jnp.bfloat16),
        hits.astype(jnp.bfloat16),
        (((1,), (1,)), ((), ())),
        preferred_element_type=jnp.float32,
    )
    flag = live[0].astype(jnp.float32)

    token_wait(1)
    token_send(2)
    from_ring(0, first, far_y, 0)
    from_ring(0, second, far_y, 0)
    for half in range(2):
        arrived(sbuf.at[:, :, rows_of(half), :], sink_recv.at[half])

    tall = 2 * rows
    lhs_real = sbuf[:, 0].reshape(NF * tall, nop * rows)
    lhs_imag = sbuf[:, 1].reshape(NF * tall, nop * rows)
    left = lax.broadcasted_iota(jnp.int32, (NF * tall, 128), 1) < 64

    def mul(a, b):
        return jnp.dot(a, b, preferred_element_type=jnp.float32)

    def multiply(b):
        for n in range(2):
            low, high = slice(n * 128, n * 128 + 128), slice(n * 128 + 256, n * 128 + 384)
            right_real = jnp.concatenate([rfull[b, 0, :, low], rfull[b, 0, :, high]], axis=-1)
            right_imag = jnp.concatenate([rfull[b, 1, :, low], rfull[b, 1, :, high]], axis=-1)
            real = mul(lhs_real, right_real) - mul(lhs_imag, right_imag)
            imag = mul(lhs_real, right_imag) + mul(lhs_imag, right_real)
            for part, value in enumerate((real, imag)):
                one, two = value[:, :128], value[:, 128:]
                even = jnp.where(left, one, pltpu.roll(two, 64, 1)).astype(jnp.bfloat16)
                odd = jnp.where(left, pltpu.roll(one, 64, 1), two).astype(jnp.bfloat16)
                prod[2 * n, b, part] = even.reshape(NF, tall, 128)
                prod[2 * n + 1, b, part] = odd.reshape(NF, tall, 128)

    blocks = []
    far_blocks = []

    def give(b):
        near_copy = send(
            prod.at[taker_y, b],
            recv.at[1, b],
            block_send.at[b],
            block_recv.at[b],
            device(z, x, core, taker_y),
        )
        far_copy = send(
            prod.at[far_y, b],
            recv.at[2, b],
            block_send.at[2 + b],
            block_recv.at[2 + b],
            device(z, x, core, far_y),
        )

        @pl.when(gives_far)
        def _():
            far_copy.start()

        near_copy.start()
        blocks.append(near_copy)
        far_blocks.append(far_copy)

    def shared(b):
        for half in range(2):
            for y_at in range(ny):
                index = b * nop + half * ny + y_at
                arrived(chunk(b, 1 - core, half, y_at), pair_recv.at[index])

    shared(0)
    multiply(0)
    from_ring(1, first, right_y, 0)
    from_ring(1, second, left_y, 0)
    give(0)
    from_ring(1, first, far_y, 0)
    from_ring(1, second, far_y, 0)
    shared(1)
    multiply(1)
    recv[0] = prod[y] * jnp.bfloat16(0.5)
    give(1)
    token_wait(2)
    token_send(3)

    order = [(part, b, a) for part in range(2) for b in range(NF) for a in range(NF)]
    own, near, far = [
        jnp.concatenate([prod[at_y, b, part, a] for part, b, a in order], axis=0)
        for at_y in (y, giver_y, far_y)
    ]
    others = jnp.concatenate([near, far], axis=1)
    place_row = lax.broadcasted_iota(jnp.int32, (8, 128), 0)
    place_lane = lax.broadcasted_iota(jnp.int32, (8, 128), 1)
    diagonal = lax.broadcasted_iota(jnp.int32, (tall, 256), 0) == lax.rem(
        lax.broadcasted_iota(jnp.int32, (tall, 256), 1), 128
    )
    total = jnp.zeros((8, 128), jnp.float32)

    def pair_of(slot, d, c):
        return jnp.concatenate([recv[slot, d, 0, c], recv[slot, d, 1, c]], axis=1)

    def traced(lhs, rhs):
        square = mul(lhs, rhs).reshape(8, tall, 256)
        return jnp.where(diagonal, square, 0.0).sum(axis=1)

    alone = [[traced(own, pair_of(0, d, c)) for c in range(NF)] for d in range(NF)]
    for d in range(NF):
        blocks[d].wait_recv()

        @pl.when(jnp.logical_not(gives_far))
        def _(d=d):
            far_blocks[d].wait_recv()

        for c in range(NF):
            right = jnp.concatenate([pair_of(1, d, c), pair_of(2, d, c)], axis=0)
            kept = alone[d][c] + traced(others, right)
            with_real, with_imag = kept[:, :128], kept[:, 128:]
            real = with_real[:4] - with_imag[4:]
            imag = with_imag[:4] + with_real[4:]
            value = jnp.concatenate([real, imag], axis=0).sum(axis=1, keepdims=True)
            slot_at = place_lane == place_row * 8 + (core * 4 + d * 2 + c)
            total = total + jnp.where(slot_at, value, 0.0)
    lane = lax.broadcasted_iota(jnp.int32, (1, 128), 1)
    row_plane[...] = total.sum(axis=0, keepdims=True) + jnp.where(
        lane == 64 + here, flag * (1.0 / nop), 0.0
    )

    def exchange(buffer, me, source, peers, index):
        buffer[me] = source[...]
        for where in peers:
            send(source, buffer.at[me], red_send.at[index], red_recv.at[index], where).start()

    def exchanged(buffer, peers, index):
        arrived(buffer.at[pl.ds(0, len(peers))], red_recv.at[index])

    def around(d, n):
        return min(d, n - d)

    spots = [(dx, dy, k) for dx in range(NX) for dy in range(ny) for k in range(2)][1:]
    spots.sort(key=lambda s: -(around(s[0], NX) + around(s[1], ny)))
    exchange(
        plane,
        x * nop + core * ny + y,
        row_plane,
        [device(z, at(x, dx, NX), at(core, k, 2), at(y, dy, ny)) for dx, dy, k in spots],
        0,
    )
    exchanged(plane, spots, 0)
    sums = [plane[j * nop : (j + 1) * nop].sum(axis=0) for j in range(NX)]
    flags = sums[0] + sums[1] + sums[2] + sums[3]
    weighted = jnp.zeros((1, 128), jnp.float32)
    for j in range(NX):
        alive = jnp.where(lane == 64 + (3 * j + 2) % 5, flags, 0.0).sum(axis=1, keepdims=True)
        weighted = weighted + alive * sums[j]
    row_z[...] = weighted

    token_wait(3)
    hops = sorted(range(1, nz), key=lambda d: -around(d, nz))
    exchange(line, z, row_z, [device(at(z, d, nz), x, core, y) for d in hops], 1)

    for copy, mine in outgoing:

        @pl.when(jnp.logical_not(mine))
        def _(copy=copy):
            copy.wait_send()

    for copy in ring + pairs + blocks:
        copy.wait_send()

    @pl.when(gives_far)
    def _():
        for copy in far_blocks:
            copy.wait_send()

    exchanged(line, hops, 1)
    everything = line[...].sum(axis=0)

    pick_row = lax.broadcasted_iota(jnp.int32, (8, 128), 0)
    pick_lane = lax.broadcasted_iota(jnp.int32, (8, 128), 1)
    picked = (pick_lane // 32 == pick_row // 2) & (
        lax.rem(pick_lane // 4, 2) == lax.rem(pick_row, 2)
    )
    spread = jnp.where(picked, everything * (1.0 / math.sqrt(ntm)), 0.0)
    result = lax.dot_general(
        spread,
        selector,
        (((1,), (1,)), ((), ())),
        precision=lax.Precision.HIGHEST,
        preferred_element_type=jnp.float32,
    )
    out_ref[...] = result[:4]

    arrived(plane.at[pl.ds(0, len(spots))], red_send.at[0])
    arrived(line.at[pl.ds(0, len(hops))], red_send.at[1])


def per_device(ntm, nop, sink, source, live, factors, target):
    rows, width = sink.shape[3], sink.shape[4]
    chains = target.shape[0]
    hbm = pl.BlockSpec(memory_space=pltpu.HBM)
    dma = pltpu.SemaphoreType.DMA
    pin = functools.partial(pltpu.with_memory_space_constraint, memory_space=pltpu.HBM)
    out = pl.pallas_call(
        functools.partial(kernel, ntm, nop),
        out_shape=jax.ShapeDtypeStruct((2 * WIN, NCORR), jnp.float32),
        in_specs=[hbm, hbm, pl.BlockSpec(memory_space=pltpu.SMEM), hbm, hbm],
        out_specs=pl.BlockSpec(memory_space=pltpu.VMEM),
        scratch_shapes=[
            pltpu.VMEM((NF, 2, width, width), jnp.bfloat16),
            pltpu.VMEM((NF, 2, 2 * rows, width), jnp.bfloat16),
            pltpu.VMEM((nop // 2, NF, 2, NF, 2 * rows, 128), jnp.bfloat16),
            pltpu.VMEM((3, NF, 2, NF, 2 * rows, 128), jnp.bfloat16),
            pltpu.VMEM((1, 128), jnp.float32),
            pltpu.VMEM((1, 128), jnp.float32),
            pltpu.VMEM((NX * nop, 1, 128), jnp.float32),
            pltpu.VMEM((ntm // NX, 1, 128), jnp.float32),
            pltpu.VMEM((4, chains), jnp.int32),
            pltpu.VMEM((1, chains), jnp.int32),
            dma((2,)),
            dma((2 * NF,)),
            dma((2 * NF,)),
            dma((WIN,)),
            dma((2,)),
            dma((6 * NF,)),
            dma((nop * NF,)),
            dma((nop * NF,)),
            dma((nop * NF,)),
            dma((4,)),
            dma((4,)),
            dma((2,)),
            dma((2,)),
            pltpu.SemaphoreType.REGULAR((8,)),
        ],
        compiler_params=pltpu.CompilerParams(
            collective_id=0, has_side_effects=True, vmem_limit_bytes=48 << 20
        ),
        name="correlate",
    )(pin(sink), pin(source), live, pin(factors.T), pin(target.reshape(1, chains)))
    return jnp.moveaxis(out.reshape(2, WIN, NCORR), 1, 2)


def solution(mesh):
    ntm, nop = mesh.shape["tm"], mesh.shape["op"]
    return jax.shard_map(
        functools.partial(per_device, ntm, nop),
        mesh=mesh,
        in_specs=(
            P("tm", None, None, "op", None),
            P("tm", None, None, "op", None),
            P("tm"),
            P(),
            P(),
        ),
        out_specs=P(),
        check_vma=False,
    )
```
